128 devices in a mesh: leaf: 16 (over z, y), panel: 8 (over x, core).
Axes of the slice: x: 4, y: 4, z: 4, core: 2. Of those that a mesh axis runs over, the one named last changes fastest.
Arguments:
- rhs: float32 [4, 16384, 256], P(None, ('leaf', 'panel')), may hold values from -6 to 6
- lower_inv: float32 [4, 16384, 128], P(None, ('leaf', 'panel')), may hold values from -0.13258252 to 1.1325825
- upper_inv: float32 [4, 16384, 128], P(None, ('leaf', 'panel')), may hold values from -0.13258252 to 1.1325825
- lower_coupling_1: float32 [2048, 16384], P(None, ('leaf', 'panel')), may hold values from -0.25 to 0.25
- lower_coupling_2: float32 [4096, 16384], P(None, ('leaf', 'panel')), may hold values from -0.1875 to 0.1875
- lower_coupling_3: float32 [8192, 16384], P(None, ('leaf', 'panel')), may hold values from -0.125 to 0.125
- upper_coupling_1: float32 [16384, 2048], P(('leaf', 'panel')), may hold values from -0.0625 to 0.0625
- upper_coupling_2: float32 [16384, 4096], P(('leaf', 'panel')), may hold values from -0.046875 to 0.046875
- upper_coupling_3: float32 [16384, 8192], P(('leaf', 'panel')), may hold values from -0.03125 to 0.03125
Outputs:
- solution: float32 [4, 16384, 256], P(None, ('leaf', 'panel'))
The draws below stay inside these ranges and needn't reach their ends.
All inputs are finite; a program needn't handle non-finite values.
Results may differ from the reference program's by a relative error of at most 0.0001.
Values sent between devices are 32-bit elements; how exact they have to be, the bound alone decides.
No kernel may reach another device: no remote copies, remote signals or barrier semaphores. Data moves between devices by JAX's collectives and lax.ppermute only.
A program may use at most 128 MiB of HBM per device.

```python
import jax
import jax.numpy as jnp
from jax import lax

BLK = 128
RHS = 256
LEVELS = 3
ROWS_ALL = 16384
N_PANEL = 8


def inverse_blocks(key):
    shape = (LEVELS + 1, ROWS_ALL, BLK)
    rowpos = lax.broadcasted_iota(jnp.int32, shape, 1) % BLK
    colpos = lax.broadcasted_iota(jnp.int32, shape, 2)
    identity = (rowpos == colpos).astype(jnp.float32)
    noise = jnp.clip(jax.random.normal(key, shape, jnp.float32), -3.0, 3.0)
    return identity + 0.5 / BLK ** 0.5 * noise


def draw_lower_inv(key, part):
    return inverse_blocks(jax.random.fold_in(key, 11))


def draw_upper_inv(key, part):
    return inverse_blocks(jax.random.fold_in(key, 23))


def strengthened(entries, own_key, source, target, shards_of, factor):
    owner, partner = [(jnp.arange(entries.shape[dim]) // (entries.shape[dim] // shards_of)).reshape([-1 if axis == dim else 1 for axis in range(entries.ndim)]) for dim in (source, target)]
    chosen = jax.random.permutation(own_key, shards_of)[partner]
    strong = (owner == chosen) | (owner == (partner + shards_of // 2) % shards_of)
    return jnp.where(strong, factor * entries, entries)


def level_of(stream_key, shape, shards, low, largest):
    def one(axis_at, blocks):
        steps = jax.random.uniform(jax.random.fold_in(jax.random.fold_in(stream_key, 6), axis_at), (blocks,), jnp.float32, low / len(shards), largest / len(shards))
        return jnp.repeat(jnp.exp(steps), shape[axis_at] // blocks).reshape((-1,) + (1,) * (len(shape) - axis_at - 1))

    level = one(*shards[0])
    for cut in shards[1:]:
        level = level * one(*cut)
    return level


def centred(key, shape, width, most, pieces=(), kind=jnp.bfloat16):
    drawn = width * jax.random.normal(key, shape, jnp.float32)
    if pieces:
        drawn = drawn * level_of(key, shape, pieces, -0.22, 0.18)
    return jnp.clip(drawn, -most, most).astype(kind)


def heavy_noise(own_key, dims, spread, limit, pieces, heavy, dtype=jnp.bfloat16):
    array = spread * jax.random.normal(own_key, dims, jnp.float32)
    if pieces:
        array = array * level_of(own_key, dims, pieces, -0.22, 0.18)
    return jnp.clip(strengthened(array, jax.random.fold_in(own_key, 3), *heavy), -limit, limit).astype(dtype)


def setup_inputs(seed: int = 0) -> dict:
    key_list = jax.random.split(jax.random.key(seed), 10)
    return {
        "rhs": centred(key_list[0], (LEVELS + 1, ROWS_ALL, RHS), 1.0, 6.0, ((1, 128),), jnp.float32),
        "lower_inv": draw_lower_inv(jax.random.fold_in(key_list[9], 71), 0),
        "upper_inv": draw_upper_inv(jax.random.fold_in(key_list[9], 71), 0),
        "lower_coupling_1": heavy_noise(key_list[3], (BLK * N_PANEL * 2, ROWS_ALL), (4 * BLK * N_PANEL * 2) ** -0.5, 0.25, ((1, 128),), (1, 0, 128, 5.5), jnp.float32),
        "lower_coupling_2": heavy_noise(key_list[4], (BLK * N_PANEL * 4, ROWS_ALL), (4 * BLK * N_PANEL * 4) ** -0.5, 0.1875, ((1, 128),), (1, 0, 128, 5.5), jnp.float32),
        "lower_coupling_3": heavy_noise(key_list[5], (BLK * N_PANEL * 8, ROWS_ALL), (4 * BLK * N_PANEL * 8) ** -0.5, 0.125, ((1, 128),), (1, 0, 128, 5.5), jnp.float32),
        "upper_coupling_1": centred(key_list[6], (ROWS_ALL, BLK * N_PANEL * 2), (4 * BLK * N_PANEL * 2) ** -0.5, 0.0625, ((0, 128),), jnp.float32),
        "upper_coupling_2": centred(key_list[7], (ROWS_ALL, BLK * N_PANEL * 4), (4 * BLK * N_PANEL * 4) ** -0.5, 0.046875, ((0, 128),), jnp.float32),
        "upper_coupling_3": centred(key_list[8], (ROWS_ALL, BLK * N_PANEL * 8), (4 * BLK * N_PANEL * 8) ** -0.5, 0.03125, ((0, 128),), jnp.float32),
    }


def blockwise(inverse, vector):
    blocks = vector.reshape(-1, BLK, RHS)
    mats = inverse.reshape(-1, BLK, BLK)
    result = jnp.einsum("dij,djr->dir", mats, blocks, precision=lax.Precision.HIGHEST, preferred_element_type=jnp.float32)
    return result.reshape(-1, RHS)


def reference(rhs, lower_inv, upper_inv, lower_coupling_1, lower_coupling_2, lower_coupling_3, upper_coupling_1, upper_coupling_2, upper_coupling_3):
    lowers = (lower_coupling_1, lower_coupling_2, lower_coupling_3)
    uppers = (upper_coupling_1, upper_coupling_2, upper_coupling_3)
    forward = [blockwise(lower_inv[0], rhs[0])]
    for level in range(1, LEVELS + 1):
        front = BLK * N_PANEL * 2 ** level
        groups = ROWS_ALL // front
        coupling = lowers[level - 1].reshape(front, groups, front)
        previous = forward[-1].reshape(groups, front, RHS)
        update = jnp.einsum("agc,gcr->gar", coupling, previous, precision=lax.Precision.HIGHEST, preferred_element_type=jnp.float32)
        forward.append(blockwise(lower_inv[level], rhs[level] - update.reshape(ROWS_ALL, RHS)))
    backward = [None] * (LEVELS + 1)
    backward[LEVELS] = blockwise(upper_inv[LEVELS], forward[LEVELS])
    for level in range(LEVELS, 0, -1):
        front = BLK * N_PANEL * 2 ** level
        groups = ROWS_ALL // front
        coupling = uppers[level - 1].reshape(groups, front, front)
        above = backward[level].reshape(groups, front, RHS)
        back = jnp.einsum("gac,gcr->gar", coupling, above, precision=lax.Precision.HIGHEST, preferred_element_type=jnp.float32)
        backward[level - 1] = blockwise(upper_inv[level - 1], forward[level - 1] - back.reshape(ROWS_ALL, RHS))
    return jnp.stack(backward)
```

```python
import jax
import jax.numpy as jnp
from jax import lax
from jax.experimental import pallas as pl
from jax.experimental.pallas import tpu as pltpu
from jax.sharding import PartitionSpec as P

LEVELS = 3
BLK = 128
NY = 4
NX = 4
HALF = 128
F32 = jnp.float32
BF16 = jnp.bfloat16
VMEM_LIMIT = 48 << 20

OFFSETS = ((1, 2), (0, 2), (1, 1), (1, 3), (0, 1), (0, 3), (1, 0))
OFFSETS_1 = OFFSETS[::-1]

CORE, ZBASE, VIDX, BLK1, KBLK1, BLK2, KBLK2 = 0, 1, 2, 6, 14, 22, 38
TABLE = 54


def route(shard, target):
    pairs = []
    for z in range(4):
        for y in range(NY):
            for x in range(NX):
                for c in range(2):
                    to = target(z, y, x, c)
                    if to is None:
                        continue
                    tz, ty, tx, tc = to
                    pairs.append(
                        (((z * NY + y) * NX + x) * 2 + c, ((tz * NY + ty) * NX + tx) * 2 + tc)
                    )
    return lax.ppermute(shard, ("leaf", "panel"), pairs)


def to_core(shard):
    return route(shard, lambda z, y, x, c: (z, y, x, 1 - c))


def to_z(shard):
    return route(shard, lambda z, y, x, c: (z ^ 1, y, x, c))


def shift_u(shard, r):
    return route(
        shard,
        lambda z, y, x, c: (z, y, (x + r) % NX, c) if c == 0 else (z, (y + r) % NY, x, c),
    )


def shift_v(shard, r):
    return route(
        shard,
        lambda z, y, x, c: (z, (y + r) % NY, x, c) if c == 0 else (z, y, (x + r) % NX, c),
    )


def near(shard, j):
    def target(z, y, x, c):
        dy, dx = OFFSETS[j] if c == 0 else OFFSETS_1[j]
        return (z, y ^ dy, (x + dx) % NX, c)

    return route(shard, target)


def split(a):
    high = a.astype(BF16)
    low = (a - high.astype(F32)).astype(BF16)
    return high, low


def paired(a):
    high, low = split(a)
    return jnp.concatenate([high, low], axis=1)


def mul(weights, pair):
    high, low = split(weights)
    r = jnp.dot(high, pair, preferred_element_type=F32)
    r = r + jnp.dot(low, pair, preferred_element_type=F32)
    return r[:, :HALF] + r[:, HALF:]


def exact(a, b):
    return jnp.dot(a, b, precision=lax.Precision.HIGHEST, preferred_element_type=F32)


def whole(a):
    n = a.ndim
    return pl.BlockSpec(a.shape, lambda i: (0,) * n)


def at_level(k):
    return lambda a: pl.BlockSpec((1,) + a.shape[1:], lambda i: (k, 0, 0))


ANY = pl.BlockSpec(memory_space=pl.ANY)
SMEM = pl.BlockSpec(memory_space=pltpu.SMEM)


def run(body, table, ins, outs, scratch=()):
    specs = [SMEM]
    for a, spec in ins:
        specs.append(spec if isinstance(spec, pl.BlockSpec) else spec(a))
    shapes = [jax.ShapeDtypeStruct(s, F32) for s in outs]
    return pl.pallas_call(
        body,
        grid=(1,),
        in_specs=specs,
        out_specs=[whole(s) for s in shapes],
        out_shape=shapes,
        scratch_shapes=list(scratch),
        compiler_params=pltpu.CompilerParams(vmem_limit_bytes=VMEM_LIMIT),
    )(table, *[a for a, _ in ins])


def half_of(ref, c):
    return jnp.where(c == 0, ref[0, :, :HALF], ref[0, :, HALF:])


def forward_step(table, finish, extra_y, sources, blocks, based):
    flat = [b for g in blocks for b in g]
    nsrc = len(sources)
    ins = []
    npiece = 0
    if finish is not None:
        level, pieces, rhs, rhs_other, inv, inv_other = finish
        npiece = len(pieces)
        ins += [(p, whole) for p in pieces]
        ins += [(a, at_level(level)) for a in (rhs, rhs_other, inv, inv_other)]
    nfin = len(ins)
    ins += [(a, whole) for a in extra_y]
    ins += [(a, ANY) for a in sources]
    outs = [(2, BLK, HALF)] if finish is not None else []
    outs += [(2, BLK, HALF) if len(g) == 1 else (len(g), 2, BLK, HALF) for g in blocks]
    nin = len(ins)

    def body(tab, *refs):
        in_refs, out_refs = refs[:nin], list(refs[nin : nin + len(outs)])
        wbuf, sems = refs[nin + len(outs) :]
        srcs = in_refs[nin - nsrc :]
        c = tab[CORE]
        copies = []
        for i, b in enumerate(flat):
            row = []
            for s in range(nsrc):
                start = tab[b] * (2 * BLK)
                if based[s]:
                    start = start + tab[ZBASE] * (NY * NX * 2 * BLK)
                start = pl.multiple_of(start, 2 * BLK)
                cp = pltpu.make_async_copy(
                    srcs[s].at[pl.ds(start, 2 * BLK), :],
                    wbuf.at[i, :, pl.ds(s * BLK, BLK)],
                    sems.at[i * nsrc + s],
                )
                cp.start()
                row.append(cp)
            copies.append(row)
        ys = []
        if finish is not None:
            pieces = in_refs[:npiece]
            rhs, rhs_other, inv, inv_other = in_refs[npiece:nfin]
            y_ref = out_refs.pop(0)
            for idx, r, m in ((c, rhs, inv), (1 - c, rhs_other, inv_other)):
                t = half_of(r, c)
                if npiece:
                    update = pieces[0][idx]
                    for p in pieces[1:]:
                        update = update + p[idx]
                    t = t - update
                y = exact(m[0], t)
                y_ref[idx] = y
                ys.append(y)
        for y_in in in_refs[nfin : nin - nsrc]:
            ys += [y_in[c], y_in[1 - c]]
        pair = paired(jnp.concatenate(ys, axis=0))
        i = 0
        for g, out in zip(blocks, out_refs):
            for n in range(len(g)):
                for cp in copies[i]:
                    cp.wait()
                r = mul(wbuf[i], pair).reshape(2, BLK, HALF)
                if len(g) == 1:
                    out[...] = r
                else:
                    out[n] = r
                i += 1

    return run(
        body,
        table,
        ins,
        outs,
        [
            pltpu.VMEM((len(flat), 2 * BLK, nsrc * BLK), F32),
            pltpu.SemaphoreType.DMA((len(flat) * nsrc,)),
        ],
    )


def sum_step(table, chunks):
    def body(tab, *refs):
        for vr in range(4):
            idx = tab[VIDX + vr]
            total = refs[0][idx]
            for r in refs[1:4]:
                total = total + r[idx]
            refs[4 + vr][...] = total

    return run(body, table, [(a, whole) for a in chunks], [(2, BLK, HALF)] * 4)


def top_step(table, pieces, rhs, rhs_other, low, low_other, up, up_other):
    n = len(pieces)

    def body(tab, *refs):
        ps = refs[:n]
        r0, r1, l0, l1, u0, u1, x_ref, mine_ref, send_ref = refs[n:]
        c = tab[CORE]
        for idx, r, lo, hi, part in ((c, r0, l0, u0, mine_ref), (1 - c, r1, l1, u1, send_ref)):
            update = ps[0][idx]
            for p in ps[1:]:
                update = update + p[idx]
            x = exact(hi[0], exact(lo[0], half_of(r, c) - update))
            x_ref[idx] = x
            part[...] = x

    level = at_level(LEVELS)
    ins = [(p, whole) for p in pieces]
    ins += [(a, level) for a in (rhs, rhs_other, low, low_other, up, up_other)]
    return run(body, table, ins, [(2, BLK, HALF), (BLK, HALF), (BLK, HALF)])


def backward_step(table, pieces, places, sources, based, finish):
    nsrc = len(sources)
    npiece = len(pieces)
    total = sum(len(p) for p in places)
    width = total * 2 * BLK
    ins = [(p, whole) for p in pieces]
    if finish is not None:
        level, y, inv, inv_other = finish
        ins += [(y, whole), (inv, at_level(level)), (inv_other, at_level(level))]
        outs = [(2, BLK, HALF), (BLK, HALF), (BLK, HALF)]
    else:
        outs = [(2, BLK, HALF)] * (nsrc // 2)
    ins += [(a, ANY) for a in sources]
    nin = len(ins)

    def body(tab, *refs):
        in_refs, out_refs = refs[:nin], refs[nin : nin + len(outs)]
        ubuf, xbuf, sems = refs[nin + len(outs) :]
        srcs = in_refs[nin - nsrc :]
        c = tab[CORE]
        copies = []
        for s in range(nsrc):
            if based[s]:
                start = pl.multiple_of(tab[ZBASE] * width, width)
                src = srcs[s].at[:, pl.ds(start, width)]
            else:
                src = srcs[s]
            cp = pltpu.make_async_copy(src, ubuf.at[s], sems.at[s])
            cp.start()
            copies.append(cp)
        for p, place in zip(in_refs[:npiece], places):
            for n, b in enumerate(place):
                piece = p[...] if len(place) == 1 else p[n]
                xbuf[tab[b]] = paired(piece.reshape(2 * BLK, HALF))
        sums = []
        for s in range(nsrc):
            copies[s].wait()
            acc = jnp.zeros((BLK, 2 * HALF), F32)
            for i in range(total):
                high, low = split(ubuf[s, :, i * 2 * BLK : (i + 1) * 2 * BLK])
                acc = acc + jnp.dot(high, xbuf[i], preferred_element_type=F32)
                acc = acc + jnp.dot(low, xbuf[i], preferred_element_type=F32)
            sums.append(acc[:, :HALF] + acc[:, HALF:])
        if finish is None:
            for s in range(nsrc):
                out_refs[s // 2][c if s % 2 == 0 else 1 - c] = sums[s]
            return
        y_ref, inv, inv_other = in_refs[npiece : npiece + 3]
        x_ref, mine_ref, send_ref = out_refs
        for idx, m, back, part in ((c, inv, sums[0], mine_ref), (1 - c, inv_other, sums[1], send_ref)):
            x = exact(m[0], y_ref[idx] - back)
            x_ref[idx] = x
            part[...] = x

    return run(
        body,
        table,
        ins,
        outs,
        [
            pltpu.VMEM((nsrc, BLK, width), F32),
            pltpu.VMEM((total, 2 * BLK, 2 * HALF), BF16),
            pltpu.SemaphoreType.DMA((nsrc,)),
        ],
    )


def solve_step(table, level, y, backs, inv, inv_other):
    n = len(backs)

    def body(tab, *refs):
        y_ref, m0, m1 = refs[:3]
        x_ref, mine_ref, send_ref = refs[3 + n :]
        c = tab[CORE]
        for idx, m, part in ((c, m0, mine_ref), (1 - c, m1, send_ref)):
            t = y_ref[idx]
            for b in refs[3 : 3 + n]:
                t = t - b[idx]
            x = exact(m[0], t)
            x_ref[idx] = x
            part[...] = x

    ins = [(y, whole), (inv, at_level(level)), (inv_other, at_level(level))]
    ins += [(b, whole) for b in backs]
    return run(body, table, ins, [(2, BLK, HALF), (BLK, HALF), (BLK, HALF)])


def assemble(table, mine, received):
    def body(tab, *refs):
        out = refs[8]
        for k in range(4):
            a, b = refs[k][...], refs[4 + k][...]
            first = tab[CORE] == 0
            out[k, :, :HALF] = jnp.where(first, a, b)
            out[k, :, HALF:] = jnp.where(first, b, a)

    ins = [(a, whole) for a in mine + received]
    return run(body, table, ins, [(4, BLK, 2 * HALF)])[0]


def make_table(leaf, panel):
    z, y = leaf // NY, leaf % NY
    x, c = panel // 2, panel % 2
    u = jnp.where(c == 0, x, y)
    v = jnp.where(c == 0, y, x)
    four = jnp.arange(4, dtype=jnp.int32)
    ur, vr = jnp.repeat(four, 4), jnp.tile(four, 4)

    def offset(k):
        a = jnp.array([o[k] for o in OFFSETS] + [0], jnp.int32)
        b = jnp.array([o[k] for o in OFFSETS_1] + [0], jnp.int32)
        return jnp.where(c == 0, a, b)

    dy, dx = offset(0), offset(1)

    def plane(up, vp):
        return jnp.where(c == 0, vp * NX + up, up * NX + vp)

    parts = [
        jnp.stack([c, z % 2]),
        (v + four) % 4,
        ((y ^ dy) & 1) * NX + (x + dx) % NX,
        ((y ^ dy) & 1) * NX + (x - dx + NX) % NX,
        plane((u + ur) % 4, vr),
        plane((u - ur + 4) % 4, (v - vr + 4) % 4),
    ]
    return jnp.concatenate([p.astype(jnp.int32) for p in parts])


def after(value, other):
    return lax.optimization_barrier((value, other))[0]


def local(
    rhs,
    lower_inv,
    upper_inv,
    lower_coupling_1,
    lower_coupling_2,
    lower_coupling_3,
    upper_coupling_1,
    upper_coupling_2,
    upper_coupling_3,
):
    leaf, panel = lax.axis_index("leaf"), lax.axis_index("panel")
    table = make_table(leaf, panel)
    zhalf = (leaf // NY) % 2

    rhs_o = to_core(rhs)
    low_o = to_core(lower_inv)
    l1_o = to_core(lower_coupling_1)
    l3_send = lax.dynamic_index_in_dim(
        lower_coupling_3.reshape(2, -1, BLK), 1 - zhalf, 0, keepdims=False
    )
    l3_z = to_z(l3_send)

    y0, *parts = forward_step(
        table,
        (0, [], rhs, rhs_o, lower_inv, low_o),
        [],
        [lower_coupling_1, l1_o],
        [[BLK1 + j] for j in range(8)],
        [False, False],
    )
    l2_o = to_core(after(lower_coupling_2, y0))
    pieces = [parts[7]] + [near(parts[j], j) for j in range(7)]

    plane = [[BLK2 + ur * 4 + v for v in range(4)] for ur in range(4)]

    def spread(parts):
        chunks = [parts[0]] + [shift_u(parts[r], r) for r in (2, 1, 3)]
        own, *sends = sum_step(table, chunks)
        return [own] + [shift_v(s, r) for r, s in zip((1, 2, 3), sends)]

    y1, *parts = forward_step(
        table,
        (1, pieces, rhs, rhs_o, lower_inv, low_o),
        [],
        [lower_coupling_2, l2_o],
        plane,
        [False, False],
    )
    l3_o = to_core(after(lower_coupling_3, y1))
    l3_zo = to_core(after(l3_z, y1))
    up_o = to_core(after(upper_inv, y1))
    pieces = spread(parts)
    u3_cols = upper_coupling_3.shape[1] // 2
    u3_send = lax.dynamic_slice_in_dim(
        after(upper_coupling_3, l3_z), (1 - zhalf) * u3_cols, u3_cols, 1
    )
    u3_z = to_z(u3_send)

    (y2,) = forward_finish(table, 2, pieces, rhs, rhs_o, lower_inv, low_o)
    y2_z = to_z(y2)
    parts = forward_step(
        table,
        None,
        [y2, y2_z],
        [lower_coupling_3, l3_o, l3_z, l3_zo],
        plane,
        [True, True, False, False],
    )
    u3_o = to_core(after(upper_coupling_3, y2))
    u2_o = to_core(after(upper_coupling_2, y2))
    u1_o = to_core(after(upper_coupling_1, y2))
    pieces = spread(parts)
    x3, mine3, send3 = top_step(table, pieces, rhs, rhs_o, lower_inv, low_o, upper_inv, up_o)
    u3_zo = to_core(after(u3_z, x3))
    got3 = to_core(send3)

    kplane = [[KBLK2 + ur * 4 + vr for vr in range(4)] for ur in range(4)]

    def collect(x):
        line = jnp.stack([x] + [shift_v(x, r) for r in (1, 2, 3)])
        return [line] + [shift_u(line, r) for r in (1, 2, 3)]

    keep, send = backward_step(
        table,
        collect(x3),
        kplane,
        [upper_coupling_3, u3_o, u3_z, u3_zo],
        [True, True, False, False],
        None,
    )
    x2, mine2, send2 = solve_step(table, 2, y2, [keep, to_z(send)], upper_inv, up_o)
    got2 = to_core(send2)
    x1, mine1, send1 = backward_step(
        table,
        collect(x2),
        kplane,
        [upper_coupling_2, u2_o],
        [False, False],
        (1, y1, upper_inv, up_o),
    )
    got1 = to_core(send1)
    gathered = [x1] + [near(x1, j) for j in range(7)]
    places = [[KBLK1 + 7]] + [[KBLK1 + j] for j in range(7)]
    _, mine0, send0 = backward_step(
        table,
        gathered,
        places,
        [upper_coupling_1, u1_o],
        [False, False],
        (0, y0, upper_inv, up_o),
    )
    got0 = to_core(send0)
    return assemble(table, [mine0, mine1, mine2, mine3], [got0, got1, got2, got3])


def forward_finish(table, level, pieces, rhs, rhs_other, inv, inv_other):
    n = len(pieces)

    def body(tab, *refs):
        ps = refs[:n]
        r0, r1, m0, m1, y_ref = refs[n:]
        c = tab[CORE]
        for idx, r, m in ((c, r0, m0), (1 - c, r1, m1)):
            update = ps[0][idx]
            for p in ps[1:]:
                update = update + p[idx]
            y_ref[idx] = exact(m[0], half_of(r, c) - update)

    ins = [(p, whole) for p in pieces]
    ins += [(a, at_level(level)) for a in (rhs, rhs_other, inv, inv_other)]
    return run(body, table, ins, [(2, BLK, HALF)])


def solution(mesh):
    return jax.shard_map(
        local,
        mesh=mesh,
        in_specs=(
            P(None, ("leaf", "panel"), None),
            P(None, ("leaf", "panel"), None),
            P(None, ("leaf", "panel"), None),
            P(None, ("leaf", "panel")),
            P(None, ("leaf", "panel")),
            P(None, ("leaf", "panel")),
            P(("leaf", "panel"), None),
            P(("leaf", "panel"), None),
            P(("leaf", "panel"), None),
        ),
        out_specs=P(None, ("leaf", "panel"), None),
        check_vma=False,
    )
```

```python
import jax
import jax.numpy as jnp
from jax import lax
from jax.experimental import pallas as pl
from jax.experimental.pallas import tpu as pltpu
from jax.sharding import PartitionSpec as P

LEVELS = 3
BLK = 128
NY = 4
NX = 4
HALF = 128
F32 = jnp.float32
BF16 = jnp.bfloat16
VMEM_LIMIT = 16 << 20

OFFSETS = ((1, 2), (0, 2), (1, 1), (1, 3), (0, 1), (0, 3), (1, 0))
OFFSETS_1 = OFFSETS[::-1]

CORE, ZBASE, VIDX, BLK1, KBLK1, BLK2, KBLK2 = 0, 1, 2, 6, 14, 22, 38
TABLE = 54


def route(shard, target):
    pairs = []
    for z in range(4):
        for y in range(NY):
            for x in range(NX):
                for c in range(2):
                    to = target(z, y, x, c)
                    if to is None:
                        continue
                    tz, ty, tx, tc = to
                    pairs.append(
                        (((z * NY + y) * NX + x) * 2 + c, ((tz * NY + ty) * NX + tx) * 2 + tc)
                    )
    return lax.ppermute(shard, ("leaf", "panel"), pairs)


def to_core(shard):
    return route(shard, lambda z, y, x, c: (z, y, x, 1 - c))


def to_z(shard):
    return route(shard, lambda z, y, x, c: (z ^ 1, y, x, c))


def shift_u(shard, r):
    return route(
        shard,
        lambda z, y, x, c: (z, y, (x + r) % NX, c) if c == 0 else (z, (y + r) % NY, x, c),
    )


def shift_v(shard, r):
    return route(
        shard,
        lambda z, y, x, c: (z, (y + r) % NY, x, c) if c == 0 else (z, y, (x + r) % NX, c),
    )


def near(shard, j):
    def target(z, y, x, c):
        dy, dx = OFFSETS[j] if c == 0 else OFFSETS_1[j]
        return (z, y ^ dy, (x + dx) % NX, c)

    return route(shard, target)


def split(a):
    high = a.astype(BF16)
    low = (a - high.astype(F32)).astype(BF16)
    return high, low


def paired(a):
    high, low = split(a)
    return jnp.concatenate([high, low], axis=1)


def wide(weights, pair):
    both = jnp.concatenate(split(weights), axis=1)
    twice = jnp.concatenate([pair, pair], axis=0)
    return jnp.dot(both, twice, preferred_element_type=F32)


def mul(weights, pair):
    r = wide(weights, pair)
    return r[:, :HALF] + r[:, HALF:]


def exact(a, b):
    return mul(a, paired(b))


WHOLE = pl.BlockSpec(memory_space=pltpu.VMEM)
HBM = pl.BlockSpec(memory_space=pl.ANY)
SMEM = pl.BlockSpec(memory_space=pltpu.SMEM)
TILE = (BLK, HALF)
PAIR = (2, BLK, HALF)


def run(body, table, ins, outs, scratch=()):
    return pl.pallas_call(
        body,
        in_specs=[SMEM] + [spec for _, spec in ins],
        out_specs=[WHOLE] * len(outs),
        out_shape=[jax.ShapeDtypeStruct(s, F32) for s in outs],
        scratch_shapes=list(scratch),
        compiler_params=pltpu.CompilerParams(vmem_limit_bytes=VMEM_LIMIT),
    )(table, *[a for a, _ in ins])


def copy(src, dst, sem):
    cp = pltpu.make_async_copy(src, dst, sem)
    cp.start()
    return cp


SMALL_SCRATCH = [
    pltpu.VMEM(PAIR, F32),
    pltpu.VMEM(PAIR, F32),
    pltpu.SemaphoreType.DMA((4,)),
]


def small_start(level, c, rhs_refs, inv_refs, scratch):
    rbuf, mbuf, sems = scratch
    copies = []
    for i, r in enumerate(rhs_refs):
        lane = pl.multiple_of(c * HALF, HALF)
        copies.append(copy(r.at[level, :, pl.ds(lane, HALF)], rbuf.at[i], sems.at[i]))
    for i, r in enumerate(inv_refs):
        copies.append(copy(r.at[level], mbuf.at[i], sems.at[2 + i]))
    return copies


def wait_all(copies):
    for cp in copies:
        cp.wait()


def fetch(refs, start, size, axis, dst, sem):
    if len(refs) == 1:
        return copy(cut(refs[0], start, size, axis), dst, sem)
    first = 0
    for ref in refs:
        past = first + ref.shape[axis]

        @pl.when((start >= first) & (start < past))
        def _(ref=ref, first=first):
            copy(cut(ref, start - first, size, axis), dst, sem)

        first = past

    return pltpu.make_async_copy(cut(refs[0], 0, size, axis), dst, sem)


def cut(ref, start, size, axis):
    if not isinstance(start, int):
        start = pl.multiple_of(start, size)
    window = pl.ds(start, size)
    return ref.at[window, :] if axis == 0 else ref.at[:, window]


def flatten(sources):
    return [a for src, _ in sources for a in src]


def regroup(sources, refs):
    out, i = [], 0
    for src, based in sources:
        out.append((refs[i : i + len(src)], based))
        i += len(src)
    return out


def start_of(tab, place, based):
    start = tab[place] * (2 * BLK)
    return start + tab[ZBASE] * (NY * NX * 2 * BLK) if based else start


def forward_step(table, finish, extra_y, sources, blocks, aside=None):
    flat = [b for g in blocks for b in g]
    nsrc = len(sources)
    ins = []
    npiece = 0
    if finish is not None:
        level, pieces, rhs, rhs_other, inv, inv_other = finish
        npiece = len(pieces)
        ins += [(p, WHOLE) for p in pieces]
        ins += [(a, HBM) for a in (rhs, rhs_other, inv, inv_other)]
    nfin = len(ins)
    ins += [(a, WHOLE) for a in extra_y]
    ny = len(ins)
    ins += [(a, HBM) for a in flatten(sources)]
    nw = len(ins)
    outs = [PAIR] if finish is not None else []
    outs += [PAIR if len(g) == 1 else (len(g),) + PAIR for g in blocks]
    if aside is not None:
        ins.append((aside[0], HBM))
        half = aside[0].shape[1] // 2
        widths = (aside[1], half - aside[1])
        outs += [(aside[0].shape[0], w) for w in widths]
    nin = len(ins)

    def body(tab, *refs):
        in_refs, out_refs = refs[:nin], list(refs[nin : nin + len(outs)])
        scratch = list(refs[nin + len(outs) :])
        c = tab[CORE]
        if aside is not None:
            base = pl.multiple_of((1 - tab[ZBASE]) * half, half)
            parts = out_refs[-2:]
            out_refs = out_refs[:-2]
            asides = [
                copy(in_refs[-1].at[:, pl.ds(base, widths[0])], parts[0], scratch[-1].at[0]),
                copy(
                    in_refs[-1].at[:, pl.ds(base + widths[0], widths[1])],
                    parts[1],
                    scratch[-1].at[1],
                ),
            ]
        if finish is not None:
            small = scratch[-3:]
            rhs_refs, inv_refs = in_refs[npiece : npiece + 2], in_refs[npiece + 2 : nfin]
            smalls = small_start(level, c, rhs_refs, inv_refs, small)
        copies = []
        if flat:
            wbuf, sems = scratch[:2]
            srcs = regroup(sources, in_refs[ny:nw])
            for i, b in enumerate(flat):
                for s, (src, based) in enumerate(srcs):
                    copies.append(
                        fetch(
                            src,
                            start_of(tab, b, based),
                            2 * BLK,
                            0,
                            wbuf.at[i, :, pl.ds(s * BLK, BLK)],
                            sems.at[i * nsrc + s],
                        )
                    )
        ys = []
        if finish is not None:
            y_ref = out_refs.pop(0)
            wait_all(smalls)
            for n, idx in enumerate((c, 1 - c)):
                t = small[0][n]
                if npiece:
                    update = in_refs[0][idx]
                    for p in in_refs[1:npiece]:
                        update = update + p[idx]
                    t = t - update
                y = exact(small[1][n], t)
                y_ref[idx] = y
                ys.append(y)
        if not flat:
            return
        for y_in in in_refs[nfin:ny]:
            ys += [y_in[c], y_in[1 - c]]
        pair = paired(jnp.concatenate(ys, axis=0))
        i = 0
        for g, out in zip(blocks, out_refs):
            n = len(g)
            wait_all(copies[i * nsrc : (i + n) * nsrc])
            r = mul(wbuf[i : i + n].reshape(n * 2 * BLK, nsrc * BLK), pair)
            out[...] = r.reshape(PAIR if n == 1 else (n,) + PAIR)
            i += n
        if aside is not None:
            wait_all(asides)

    scratch = []
    if flat:
        scratch += [
            pltpu.VMEM((len(flat), 2 * BLK, nsrc * BLK), F32),
            pltpu.SemaphoreType.DMA((len(flat) * nsrc,)),
        ]
    if finish is not None:
        scratch += SMALL_SCRATCH
    if aside is not None:
        scratch.append(pltpu.SemaphoreType.DMA((2,)))
    return run(body, table, ins, outs, scratch)


def pick(table, source, size, axis, place, flip):
    shape = list(source.shape)
    shape[axis] = size

    def body(tab, src, out, sem):
        part = 1 - tab[place] if flip else tab[place]
        copy(cut(src, part * size, size, axis), out, sem).wait()

    return run(body, table, [(source, HBM)], [tuple(shape)], [pltpu.SemaphoreType.DMA])[0]


def sum_step(table, chunks, waits=()):
    n = 4 + len(waits)

    def body(tab, *refs):
        for vr in range(4):
            idx = tab[VIDX + vr]
            total = refs[0][idx]
            for r in refs[1:4]:
                total = total + r[idx]
            refs[n + vr][...] = total

    ins = [(a, WHOLE) for a in chunks] + [(a, HBM) for a in waits]
    return run(body, table, ins, [PAIR] * 4)


def top_step(table, pieces, rhs, rhs_other, low, low_other, up, up_other):
    n = len(pieces)

    def body(tab, *refs):
        r0, r1, l0, l1, u0, u1, x_ref, mine_ref, send_ref = refs[n : n + 9]
        rbuf, mbuf, sems, ubuf, usems = refs[n + 9 :]
        c = tab[CORE]
        copies = small_start(LEVELS, c, (r0, r1), (l0, l1), (rbuf, mbuf, sems))
        for i, r in enumerate((u0, u1)):
            copies.append(copy(r.at[LEVELS], ubuf.at[i], usems.at[i]))
        wait_all(copies)
        for i, (idx, part) in enumerate(((c, mine_ref), (1 - c, send_ref))):
            update = refs[0][idx]
            for p in refs[1:n]:
                update = update + p[idx]
            x = exact(ubuf[i], exact(mbuf[i], rbuf[i] - update))
            x_ref[idx] = x
            part[...] = x

    ins = [(p, WHOLE) for p in pieces]
    ins += [(a, HBM) for a in (rhs, rhs_other, low, low_other, up, up_other)]
    scratch = SMALL_SCRATCH + [pltpu.VMEM(PAIR, F32), pltpu.SemaphoreType.DMA((2,))]
    return run(body, table, ins, [PAIR, TILE, TILE], scratch)


def backward_step(table, before, pieces, places, sources, finish, paired_out=False, waits=()):
    nsrc = len(sources)
    npiece = len(pieces)
    flat = [b for p in places for b in p]
    nblk = len(flat)
    ins = [(p, WHOLE) for p in pieces]
    if before is not None:
        ins.append((before, WHOLE))
    nacc = len(ins)
    if finish is not None:
        level, y, inv, inv_other = finish
        ins += [(y, WHOLE), (inv, HBM), (inv_other, HBM)]
        outs = [PAIR, TILE, TILE]
    elif paired_out:
        outs = [PAIR] * (nsrc // 2)
    else:
        outs = [(nsrc * BLK, HALF)]
    nf = len(ins)
    ins += [(a, HBM) for a in flatten(sources)]
    nw = len(ins)
    ins += [(a, HBM) for a in waits]
    nin = len(ins)

    def body(tab, *refs):
        in_refs, out_refs = refs[:nin], refs[nin : nin + len(outs)]
        ubuf, sems = refs[nin + len(outs) : nin + len(outs) + 2]
        srcs = regroup(sources, in_refs[nf:nw])
        c = tab[CORE]
        copies = []
        for i, b in enumerate(flat):
            for s, (src, based) in enumerate(srcs):
                copies.append(
                    fetch(
                        src,
                        start_of(tab, b, based),
                        2 * BLK,
                        1,
                        ubuf.at[i, pl.ds(s * BLK, BLK), :],
                        sems.at[i * nsrc + s],
                    )
                )
        if finish is not None:
            small = refs[nin + len(outs) + 2 :]
            smalls = small_start(level, c, (), in_refs[nacc + 1 : nf], small)
        total = None
        i = 0
        for p, place in zip(in_refs[:npiece], places):
            for n in range(len(place)):
                piece = p[...] if len(place) == 1 else p[n]
                pair = paired(piece.reshape(2 * BLK, HALF))
                wait_all(copies[i * nsrc : (i + 1) * nsrc])
                r = wide(ubuf[i], pair)
                total = r if total is None else total + r
                i += 1
        total = total[:, :HALF] + total[:, HALF:]
        if before is not None:
            total = total + in_refs[npiece][...]
        if finish is not None:
            x_ref, mine_ref, send_ref = out_refs
            y_ref = in_refs[nacc]
            wait_all(smalls)
            for n, (idx, part) in enumerate(((c, mine_ref), (1 - c, send_ref))):
                x = exact(small[1][n], y_ref[idx] - total[n * BLK : (n + 1) * BLK])
                x_ref[idx] = x
                part[...] = x
        elif paired_out:
            for s in range(nsrc):
                idx = c if s % 2 == 0 else 1 - c
                out_refs[s // 2][idx] = total[s * BLK : (s + 1) * BLK]
        else:
            out_refs[0][...] = total

    scratch = [
        pltpu.VMEM((nblk, nsrc * BLK, 2 * BLK), F32),
        pltpu.SemaphoreType.DMA((nblk * nsrc,)),
    ]
    if finish is not None:
        scratch += SMALL_SCRATCH
    return run(body, table, ins, outs, scratch)


def solve_step(table, level, y, backs, inv, inv_other):
    n = len(backs)

    def body(tab, *refs):
        y_ref, m0, m1 = refs[:3]
        x_ref, mine_ref, send_ref = refs[3 + n : 6 + n]
        small = refs[6 + n :]
        c = tab[CORE]
        wait_all(small_start(level, c, (), (m0, m1), small))
        for i, (idx, part) in enumerate(((c, mine_ref), (1 - c, send_ref))):
            t = y_ref[idx]
            for b in refs[3 : 3 + n]:
                t = t - b[idx]
            x = exact(small[1][i], t)
            x_ref[idx] = x
            part[...] = x

    ins = [(y, WHOLE), (inv, HBM), (inv_other, HBM)]
    ins += [(b, WHOLE) for b in backs]
    return run(body, table, ins, [PAIR, TILE, TILE], SMALL_SCRATCH)


def assemble(table, mine, received):
    def body(tab, *refs):
        out = refs[8]
        for k in range(4):
            a, b = refs[k][...], refs[4 + k][...]
            first = tab[CORE] == 0
            out[k, :, :HALF] = jnp.where(first, a, b)
            out[k, :, HALF:] = jnp.where(first, b, a)

    ins = [(a, WHOLE) for a in mine + received]
    return run(body, table, ins, [(4, BLK, 2 * HALF)])[0]


def make_table(leaf, panel):
    z, y = leaf // NY, leaf % NY
    x, c = panel // 2, panel % 2
    u = jnp.where(c == 0, x, y)
    v = jnp.where(c == 0, y, x)
    four = jnp.arange(4, dtype=jnp.int32)
    ur, vr = jnp.repeat(four, 4), jnp.tile(four, 4)

    def offset(k):
        a = jnp.array([o[k] for o in OFFSETS] + [0], jnp.int32)
        b = jnp.array([o[k] for o in OFFSETS_1] + [0], jnp.int32)
        return jnp.where(c == 0, a, b)

    dy, dx = offset(0), offset(1)

    def plane(up, vp):
        return jnp.where(c == 0, vp * NX + up, up * NX + vp)

    parts = [
        jnp.stack([c, z % 2]),
        (v + four) % 4,
        ((y ^ dy) & 1) * NX + (x + dx) % NX,
        ((y ^ dy) & 1) * NX + (x - dx + NX) % NX,
        plane((u + ur) % 4, vr),
        plane((u - ur + 4) % 4, (v - vr + 4) % 4),
    ]
    return jnp.concatenate([p.astype(jnp.int32) for p in parts])


def after(value, other):
    return lax.optimization_barrier((value, other))[0]


U_ORDER = (1, 3, 2)
Z_PAIRS = [[i, i ^ NY] for i in range(4 * NY) if i & NY == 0]


def gather_z(shard):
    return lax.all_gather(shard, "leaf", axis_index_groups=Z_PAIRS)


def local(
    rhs,
    lower_inv,
    upper_inv,
    lower_coupling_1,
    lower_coupling_2,
    lower_coupling_3,
    upper_coupling_1,
    upper_coupling_2,
    upper_coupling_3,
):
    leaf, panel = lax.axis_index("leaf"), lax.axis_index("panel")
    table = make_table(leaf, panel)

    rhs_o = to_core(rhs)
    low_o = to_core(lower_inv)
    l1_o = to_core(lower_coupling_1)
    lows = (rhs, rhs_o, lower_inv, low_o)

    rows = lower_coupling_3.shape[0] // 2
    cols = upper_coupling_3.shape[1] // 2
    l3_send = pick(table, after(lower_coupling_3, rhs_o), rows, 0, ZBASE, True)
    l3_pair = gather_z(l3_send)

    y0, *parts = forward_step(
        table,
        (0, []) + lows,
        [],
        [([lower_coupling_1], False), ([l1_o], False)],
        [[BLK1 + j] for j in range(8)],
    )
    l2_o = to_core(after(lower_coupling_2, y0))
    pieces = [parts[7]] + [near(parts[j], j) for j in range(7)]

    plane = [[BLK2 + ur * 4 + v for v in range(4)] for ur in range(4)]

    def spread(chunks, waits=()):
        arrived = [chunks[0]] + [shift_u(chunks[r], r) for r in U_ORDER]
        own, *sends = sum_step(table, arrived, waits)
        return [own] + [shift_v(s, r) for r, s in zip((1, 2, 3), sends)]

    sources = [([lower_coupling_2], False), ([l2_o], False)]
    y1, c1, c3, c2 = forward_step(
        table, (1, pieces) + lows, [], sources, [plane[1], plane[3], plane[2]]
    )
    c0, u3_send, u3_last = forward_step(
        table, None, [y1], sources, [plane[0]], (upper_coupling_3, cols // 4 * 3)
    )
    u3_pair = gather_z(u3_send)
    l3_o = to_core(after(lower_coupling_3, y1))
    up_o = to_core(after(upper_inv, y1))
    pieces = spread([c0, c1, c2, c3])

    (y2,) = forward_step(table, (2, pieces) + lows, [], [], [])
    y2_z = to_z(y2)
    l3_z = pick(table, after(l3_pair, y2).reshape(2 * rows, BLK), rows, 0, ZBASE, True)
    l3_zo = to_core(l3_z)
    sources = [
        ([lower_coupling_3], True),
        ([l3_o], True),
        ([l3_z], False),
        ([l3_zo], False),
    ]
    c1, c3, c2 = forward_step(
        table, None, [y2, y2_z], sources, [plane[1], plane[3], plane[2]]
    )
    (c0,) = forward_step(table, None, [y2, y2_z], sources, [plane[0]])
    u3_zlast = to_z(after(u3_last, y2_z))
    u3_o = to_core(after(upper_coupling_3, y2))
    u2_o = to_core(after(upper_coupling_2, y2))
    u1_o = to_core(after(upper_coupling_1, y2))
    pieces = spread([c0, c1, c2, c3], [u3_zlast])
    x3, mine3, send3 = top_step(table, pieces, *lows, upper_inv, up_o)
    got3 = to_core(send3)

    kplane = [[KBLK2 + ur * 4 + vr for vr in range(4)] for ur in range(4)]

    def collect(x):
        line = jnp.stack([x] + [shift_v(x, r) for r in (1, 2, 3)])
        return [line] + [shift_u(line, r) for r in (1, 2, 3)]

    line, p1, p2, p3 = collect(x3)
    u3_z = pick(table, after(u3_pair, line).reshape(2 * BLK, -1), BLK, 0, ZBASE, True)
    sources = [
        ([upper_coupling_3], True),
        ([u3_o], True),
        ([u3_z, u3_zlast], False),
        ([to_core(u3_z), to_core(after(u3_zlast, x3))], False),
    ]
    (acc,) = backward_step(table, None, [line], [kplane[0]], sources, None)
    (acc,) = backward_step(table, acc, [p1], [kplane[1]], sources, None)
    keep, send = backward_step(
        table, acc, [p3, p2], [kplane[3], kplane[2]], sources, None, paired_out=True
    )
    x2, mine2, send2 = solve_step(table, 2, y2, [keep, to_z(send)], upper_inv, up_o)
    got2 = to_core(send2)

    line, p1, p2, p3 = collect(x2)
    sources = [([upper_coupling_2], False), ([u2_o], False)]
    (acc,) = backward_step(table, None, [line], [kplane[0]], sources, None)
    (acc,) = backward_step(table, acc, [p1], [kplane[1]], sources, None)
    x1, mine1, send1 = backward_step(
        table, acc, [p3, p2], [kplane[3], kplane[2]], sources, (1, y1, upper_inv, up_o)
    )
    got1 = to_core(send1)

    sources = [([upper_coupling_1], False), ([u1_o], False)]
    arrivals = [near(x1, j) for j in range(7)]
    (acc,) = backward_step(table, None, [x1], [[KBLK1 + 7]], sources, None)
    (acc,) = backward_step(
        table, acc, arrivals[:4], [[KBLK1 + j] for j in range(4)], sources, None
    )
    _, mine0, send0 = backward_step(
        table,
        acc,
        arrivals[4:],
        [[KBLK1 + j] for j in range(4, 7)],
        sources,
        (0, y0, upper_inv, up_o),
    )
    got0 = to_core(send0)
    return assemble(table, [mine0, mine1, mine2, mine3], [got0, got1, got2, got3])


def solution(mesh):
    return jax.shard_map(
        local,
        mesh=mesh,
        in_specs=(
            P(None, ("leaf", "panel"), None),
            P(None, ("leaf", "panel"), None),
            P(None, ("leaf", "panel"), None),
            P(None, ("leaf", "panel")),
            P(None, ("leaf", "panel")),
            P(None, ("leaf", "panel")),
            P(("leaf", "panel"), None),
            P(("leaf", "panel"), None),
            P(("leaf", "panel"), None),
        ),
        out_specs=P(None, ("leaf", "panel"), None),
        check_vma=False,
    )
```

```python
import jax
import jax.numpy as jnp
from jax import lax
from jax.experimental import pallas as pl
from jax.experimental.pallas import tpu as pltpu
from jax.sharding import PartitionSpec as P

LEVELS = 3
BLK = 128
NY = 4
NX = 4
HALF = 128
F32 = jnp.float32
BF16 = jnp.bfloat16
VMEM_LIMIT = 16 << 20

OFFSETS = ((1, 2), (0, 2), (1, 1), (1, 3), (0, 1), (0, 3), (1, 0))
OFFSETS_1 = OFFSETS[::-1]

CORE, ZBASE, VIDX, BLK1, KBLK1, BLK2, KBLK2 = 0, 1, 2, 6, 14, 22, 38
TABLE = 54


def route(shard, target):
    pairs = []
    for z in range(4):
        for y in range(NY):
            for x in range(NX):
                for c in range(2):
                    to = target(z, y, x, c)
                    if to is None:
                        continue
                    tz, ty, tx, tc = to
                    pairs.append(
                        (((z * NY + y) * NX + x) * 2 + c, ((tz * NY + ty) * NX + tx) * 2 + tc)
                    )
    return lax.ppermute(shard, ("leaf", "panel"), pairs)


def to_core(shard):
    return route(shard, lambda z, y, x, c: (z, y, x, 1 - c))


def to_z(shard):
    return route(shard, lambda z, y, x, c: (z ^ 1, y, x, c))


def shift_u(shard, r):
    return route(
        shard,
        lambda z, y, x, c: (z, y, (x + r) % NX, c) if c == 0 else (z, (y + r) % NY, x, c),
    )


def shift_v(shard, r):
    return route(
        shard,
        lambda z, y, x, c: (z, (y + r) % NY, x, c) if c == 0 else (z, y, (x + r) % NX, c),
    )


def near(shard, j):
    def target(z, y, x, c):
        dy, dx = OFFSETS[j] if c == 0 else OFFSETS_1[j]
        return (z, y ^ dy, (x + dx) % NX, c)

    return route(shard, target)


def split(a):
    high = a.astype(BF16)
    low = (a - high.astype(F32)).astype(BF16)
    return high, low


def paired(a):
    high, low = split(a)
    return jnp.concatenate([high, low], axis=1)


def mul(weights, pair):
    both = jnp.concatenate(split(weights), axis=1)
    twice = jnp.concatenate([pair, pair], axis=0)
    r = jnp.dot(both, twice, preferred_element_type=F32)
    return r[:, :HALF] + r[:, HALF:]


def exact(a, b):
    return mul(a, paired(b))


WHOLE = pl.BlockSpec(memory_space=pltpu.VMEM)
HBM = pl.BlockSpec(memory_space=pl.ANY)
SMEM = pl.BlockSpec(memory_space=pltpu.SMEM)
TILE = (BLK, HALF)
PAIR = (2, BLK, HALF)


def run(body, table, ins, outs, scratch=()):
    return pl.pallas_call(
        body,
        in_specs=[SMEM] + [spec for _, spec in ins],
        out_specs=[WHOLE] * len(outs),
        out_shape=[jax.ShapeDtypeStruct(s, F32) for s in outs],
        scratch_shapes=list(scratch),
        compiler_params=pltpu.CompilerParams(vmem_limit_bytes=VMEM_LIMIT),
    )(table, *[a for a, _ in ins])


def copy(src, dst, sem):
    cp = pltpu.make_async_copy(src, dst, sem)
    cp.start()
    return cp


SMALL_SCRATCH = [
    pltpu.VMEM(PAIR, F32),
    pltpu.VMEM(PAIR, F32),
    pltpu.SemaphoreType.DMA((4,)),
]


def small_start(level, c, rhs_refs, inv_refs, scratch):
    rbuf, mbuf, sems = scratch
    copies = []
    for i, r in enumerate(rhs_refs):
        lane = pl.multiple_of(c * HALF, HALF)
        copies.append(copy(r.at[level, :, pl.ds(lane, HALF)], rbuf.at[i], sems.at[i]))
    for i, r in enumerate(inv_refs):
        copies.append(copy(r.at[level], mbuf.at[i], sems.at[2 + i]))
    return copies


def wait_all(copies):
    for cp in copies:
        cp.wait()


def cut(ref, start, size, axis):
    if not isinstance(start, int):
        start = pl.multiple_of(start, size)
    window = pl.ds(start, size)
    return ref.at[window, :] if axis == 0 else ref.at[:, window]


def start_of(tab, block):
    place, half = block
    number = tab[place]
    if half:
        number = number + NY * NX * (tab[ZBASE] if half == 1 else 1 - tab[ZBASE])
    return number * (2 * BLK)


def forward_step(table, finish, extra_y, sources, blocks):
    flat = [b for g in blocks for b in g]
    nsrc = len(sources)
    ins = []
    npiece = 0
    if finish is not None:
        level, pieces, rhs, rhs_other, inv, inv_other = finish
        npiece = len(pieces)
        ins += [(p, WHOLE) for p in pieces]
        ins += [(a, HBM) for a in (rhs, rhs_other, inv, inv_other)]
    nfin = len(ins)
    ins += [(a, WHOLE) for a in extra_y]
    ny = len(ins)
    ins += [(a, HBM) for a in sources]
    nin = len(ins)
    outs = [PAIR] if finish is not None else []
    outs += [PAIR if len(g) == 1 else (len(g),) + PAIR for g in blocks]

    def body(tab, *refs):
        in_refs, out_refs = refs[:nin], list(refs[nin : nin + len(outs)])
        scratch = list(refs[nin + len(outs) :])
        c = tab[CORE]
        if finish is not None:
            small = scratch[-3:]
            rhs_refs, inv_refs = in_refs[npiece : npiece + 2], in_refs[npiece + 2 : nfin]
            smalls = small_start(level, c, rhs_refs, inv_refs, small)
        copies = []
        if flat:
            wbuf, sems = scratch[:2]
            for i, b in enumerate(flat):
                for s, src in enumerate(in_refs[ny:]):
                    copies.append(
                        copy(
                            cut(src, start_of(tab, b), 2 * BLK, 0),
                            wbuf.at[i, :, pl.ds(s * BLK, BLK)],
                            sems.at[i * nsrc + s],
                        )
                    )
        ys = []
        if finish is not None:
            y_ref = out_refs.pop(0)
            wait_all(smalls)
            for n, idx in enumerate((c, 1 - c)):
                t = small[0][n]
                if npiece:
                    update = in_refs[0][idx]
                    for p in in_refs[1:npiece]:
                        update = update + p[idx]
                    t = t - update
                y = exact(small[1][n], t)
                y_ref[idx] = y
                ys.append(y)
        if not flat:
            return
        for y_in in in_refs[nfin:ny]:
            ys += [y_in[c], y_in[1 - c]]
        pair = paired(jnp.concatenate(ys, axis=0))
        i = 0
        for g, out in zip(blocks, out_refs):
            n = len(g)
            wait_all(copies[i * nsrc : (i + n) * nsrc])
            r = mul(wbuf[i : i + n].reshape(n * 2 * BLK, nsrc * BLK), pair)
            out[...] = r.reshape(out.shape)
            i += n

    scratch = []
    if flat:
        scratch += [
            pltpu.VMEM((len(flat), 2 * BLK, nsrc * BLK), F32),
            pltpu.SemaphoreType.DMA((len(flat) * nsrc,)),
        ]
    if finish is not None:
        scratch += SMALL_SCRATCH
    return run(body, table, ins, outs, scratch)


def sum_step(table, first, second):
    n, m = len(first), len(second)
    zs = first[0].shape[0] == 4
    outs = [(2,) + PAIR if zs else PAIR] * 4

    def body(tab, *refs):
        a, b, out = refs[:n], refs[n : n + m], refs[n + m : n + m + 4]
        if zs:
            for vr in range(4):
                idx = tab[VIDX + vr]
                for half, parts in enumerate((a, b)):
                    total = parts[0][idx]
                    for p in parts[1:]:
                        total = total + p[idx]
                    out[vr][half] = total
            return
        buf = refs[-1]
        for half, parts in enumerate((a, b)):
            total = parts[0][...]
            for p in parts[1:]:
                total = total + p[...]
            buf[2 * half : 2 * half + 2] = total
        for vr in range(4):
            out[vr][...] = buf[tab[VIDX + vr]]

    ins = [(p, WHOLE) for p in first + second]
    return run(body, table, ins, outs, [] if zs else [pltpu.VMEM((4,) + PAIR, F32)])


def add_step(table, pairs):
    n = len(pairs)

    def body(tab, *refs):
        for i in range(n):
            refs[2 * n + i][...] = refs[2 * i][...] + refs[2 * i + 1][...]

    ins = [(a, WHOLE) for p in pairs for a in p]
    return run(body, table, ins, [p[0].shape for p in pairs])


def cross_step(table, pieces):
    n = len(pieces)

    def body(tab, *refs):
        for half in range(2):
            total = refs[0][half]
            for p in refs[1:n]:
                total = total + p[half]
            refs[n + half][...] = total

    return run(body, table, [(p, WHOLE) for p in pieces], [PAIR, PAIR])


def top_step(table, pieces, rhs, rhs_other, low, low_other, up, up_other):
    n = len(pieces)

    def body(tab, *refs):
        r0, r1, l0, l1, u0, u1, x_ref, mine_ref, send_ref = refs[n : n + 9]
        rbuf, mbuf, sems, ubuf, usems = refs[n + 9 :]
        c = tab[CORE]
        copies = small_start(LEVELS, c, (r0, r1), (l0, l1), (rbuf, mbuf, sems))
        for i, r in enumerate((u0, u1)):
            copies.append(copy(r.at[LEVELS], ubuf.at[i], usems.at[i]))
        wait_all(copies)
        for i, (idx, part) in enumerate(((c, mine_ref), (1 - c, send_ref))):
            update = refs[0][idx]
            for p in refs[1:n]:
                update = update + p[idx]
            x = exact(ubuf[i], exact(mbuf[i], rbuf[i] - update))
            x_ref[idx] = x
            part[...] = x

    ins = [(p, WHOLE) for p in pieces]
    ins += [(a, HBM) for a in (rhs, rhs_other, low, low_other, up, up_other)]
    scratch = SMALL_SCRATCH + [pltpu.VMEM(PAIR, F32), pltpu.SemaphoreType.DMA((2,))]
    return run(body, table, ins, [PAIR, TILE, TILE], scratch)


def backward_step(table, before, pieces, places, sources, finish):
    nsrc = len(sources)
    npiece = len(pieces)
    flat = [b for p in places for b in p]
    nblk = len(flat)
    ins = [(p, WHOLE) for p in pieces]
    if before is not None:
        ins.append((before, WHOLE))
    nacc = len(ins)
    if finish is not None:
        level, y, inv, inv_other = finish
        ins += [(y, WHOLE), (inv, HBM), (inv_other, HBM)]
        outs = [PAIR, TILE, TILE]
    else:
        outs = [(nsrc * BLK, HALF)]
    nf = len(ins)
    ins += [(a, HBM) for a in sources]
    nin = len(ins)

    def body(tab, *refs):
        in_refs, out_refs = refs[:nin], refs[nin : nin + len(outs)]
        ubuf, sems = refs[nin + len(outs) : nin + len(outs) + 2]
        c = tab[CORE]
        copies = []
        for i, b in enumerate(flat):
            for s, src in enumerate(in_refs[nf:]):
                copies.append(
                    copy(
                        cut(src, start_of(tab, b), 2 * BLK, 1),
                        ubuf.at[pl.ds(s * BLK, BLK), pl.ds(i * 2 * BLK, 2 * BLK)],
                        sems.at[i * nsrc + s],
                    )
                )
        if finish is not None:
            small = refs[nin + len(outs) + 2 :]
            smalls = small_start(level, c, (), in_refs[nacc + 1 : nf], small)
        rows = [p[...].reshape(-1, HALF) for p in in_refs[:npiece]]
        pair = paired(jnp.concatenate(rows, axis=0))
        wait_all(copies)
        high, low = split(ubuf[...])
        total = jnp.dot(high, pair, preferred_element_type=F32)
        total = total + jnp.dot(low, pair, preferred_element_type=F32)
        total = total[:, :HALF] + total[:, HALF:]
        if before is not None:
            total = total + in_refs[npiece][...]
        if finish is None:
            out_refs[0][...] = total
            return
        x_ref, mine_ref, send_ref = out_refs
        y_ref = in_refs[nacc]
        wait_all(smalls)
        for n, (idx, part) in enumerate(((c, mine_ref), (1 - c, send_ref))):
            x = exact(small[1][n], y_ref[idx] - total[n * BLK : (n + 1) * BLK])
            x_ref[idx] = x
            part[...] = x

    scratch = [
        pltpu.VMEM((nsrc * BLK, nblk * 2 * BLK), F32),
        pltpu.SemaphoreType.DMA((nblk * nsrc,)),
    ]
    if finish is not None:
        scratch += SMALL_SCRATCH
    return run(body, table, ins, outs, scratch)


def assemble(table, mine, received):
    def body(tab, *refs):
        out = refs[8]
        for k in range(4):
            a, b = refs[k][...], refs[4 + k][...]
            first = tab[CORE] == 0
            out[k, :, :HALF] = jnp.where(first, a, b)
            out[k, :, HALF:] = jnp.where(first, b, a)

    ins = [(a, WHOLE) for a in mine + received]
    return run(body, table, ins, [(4, BLK, 2 * HALF)])[0]


def make_table(leaf, panel):
    z, y = leaf // NY, leaf % NY
    x, c = panel // 2, panel % 2
    u = jnp.where(c == 0, x, y)
    v = jnp.where(c == 0, y, x)
    four = jnp.arange(4, dtype=jnp.int32)
    ur, vr = jnp.repeat(four, 4), jnp.tile(four, 4)

    def offset(k):
        a = jnp.array([o[k] for o in OFFSETS] + [0], jnp.int32)
        b = jnp.array([o[k] for o in OFFSETS_1] + [0], jnp.int32)
        return jnp.where(c == 0, a, b)

    dy, dx = offset(0), offset(1)

    def plane(up, vp):
        return jnp.where(c == 0, vp * NX + up, up * NX + vp)

    parts = [
        jnp.stack([c, z % 2]),
        (v + four) % 4,
        ((y ^ dy) & 1) * NX + (x + dx) % NX,
        ((y ^ dy) & 1) * NX + (x - dx + NX) % NX,
        plane((u + ur) % 4, vr),
        plane((u - ur + 4) % 4, (v - vr + 4) % 4),
    ]
    return jnp.concatenate([p.astype(jnp.int32) for p in parts])


def after(value, other):
    return lax.optimization_barrier((value, other))[0]


def local(
    rhs,
    lower_inv,
    upper_inv,
    lower_coupling_1,
    lower_coupling_2,
    lower_coupling_3,
    upper_coupling_1,
    upper_coupling_2,
    upper_coupling_3,
):
    leaf, panel = lax.axis_index("leaf"), lax.axis_index("panel")
    table = make_table(leaf, panel)

    rhs_o = to_core(rhs)
    low_o = to_core(lower_inv)
    l1_o = to_core(lower_coupling_1)
    lows = (rhs, rhs_o, lower_inv, low_o)
    y0, *parts = forward_step(
        table,
        (0, []) + lows,
        [],
        [lower_coupling_1, l1_o],
        [[(BLK1 + j, 0)] for j in range(8)],
    )
    l2_o = to_core(after(lower_coupling_2, y0))
    pieces = [parts[7]] + [near(parts[j], j) for j in range(7)]

    def spread(finish, ys, sources, first, second):
        out = forward_step(table, finish, ys, sources, [first[2], second[2]])
        a2, b2 = shift_u(out[-2], 1), shift_u(out[-1], -1)
        if finish is not None:
            ys = [out[0]]
        d1, d3 = forward_step(table, None, ys, sources, [second[1], first[3]])
        d1, d3 = shift_u(d1, 1), shift_u(d3, -1)
        s1, s3 = forward_step(table, None, ys, sources, [first[1], second[3]])
        s1, s3 = add_step(table, [(s1, a2), (s3, b2)])
        s1, s3 = shift_u(s1, 1), shift_u(s3, -1)
        a0, b0 = forward_step(table, None, ys, sources, [first[0], second[0]])
        own, *sends = sum_step(table, [a0, d3, s1], [b0, d1, s3])
        return ys[0], [own] + [shift_v(p, r) for r, p in zip((1, 2, 3), sends)]

    def half_plane(base, columns, z):
        return [[(base + ur * 4 + v, z) for v in columns] for ur in range(4)]

    y1, pieces = spread(
        (1, pieces) + lows,
        [],
        [lower_coupling_2, l2_o],
        half_plane(BLK2, (0, 1), 0),
        half_plane(BLK2, (2, 3), 0),
    )
    l3_o = to_core(after(lower_coupling_3, y1))
    up_o = to_core(after(upper_inv, y1))
    (y2,) = forward_step(table, (2, pieces) + lows, [], [], [])
    _, pieces = spread(
        None,
        [y2],
        [lower_coupling_3, l3_o],
        half_plane(BLK2, range(4), 1),
        half_plane(BLK2, range(4), 2),
    )
    u3_o = to_core(after(upper_coupling_3, y2))
    own, other = cross_step(table, pieces)
    x3, mine3, send3 = top_step(
        table, [own, to_z(other)], *lows, upper_inv, up_o
    )
    got3 = to_core(send3)
    u2_o = to_core(after(upper_coupling_2, x3))

    def along_v(x):
        return [x] + [shift_v(x, r) for r in (1, 2, 3)]

    def around(a, b):
        a1, b3 = shift_u(a, 1), shift_u(b, -1)
        b1, a3 = shift_u(b, 1), shift_u(a, -1)
        a2, b2 = shift_u(a1, 1), shift_u(b3, -1)
        return [(a, b), (a1, b1), (a2, b2), (a3, b3)]

    def gathered(rings, first, second, sources, finish):
        acc = None
        for urs, last in (((0,), None), ((1, 3), None), ((2,), finish)):
            arrays, places = [], []
            for ur in urs:
                arrays += rings[ur]
                places += [first[ur], second[ur]]
            out = backward_step(table, acc, arrays, places, sources, last)
            acc = out[0]
        return out

    line = along_v(jnp.stack([x3, to_z(x3)]))
    rings = around(jnp.concatenate(line[:2]), jnp.concatenate(line[2:]))
    both = [[[(KBLK2 + ur * 4 + v, z) for v in vs for z in (1, 2)] for ur in range(4)]
            for vs in ((0, 1), (2, 3))]
    x2, mine2, send2 = gathered(
        rings,
        *both,
        [upper_coupling_3, u3_o],
        (2, y2, upper_inv, up_o),
    )
    got2 = to_core(send2)
    u1_o = to_core(after(upper_coupling_1, x2))
    line = along_v(x2)
    rings = around(jnp.stack(line[:2]), jnp.stack(line[2:]))
    x1, mine1, send1 = gathered(
        rings,
        half_plane(KBLK2, (0, 1), 0),
        half_plane(KBLK2, (2, 3), 0),
        [upper_coupling_2, u2_o],
        (1, y1, upper_inv, up_o),
    )
    got1 = to_core(send1)

    sources = [upper_coupling_1, u1_o]
    arrivals = [near(x1, j) for j in range(7)]
    places = [[(KBLK1 + j, 0)] for j in range(8)]
    (acc,) = backward_step(table, None, [x1], places[7:], sources, None)
    (acc,) = backward_step(table, acc, arrivals[:4], places[:4], sources, None)
    _, mine0, send0 = backward_step(
        table, acc, arrivals[4:], places[4:7], sources, (0, y0, upper_inv, up_o)
    )
    got0 = to_core(send0)
    return assemble(table, [mine0, mine1, mine2, mine3], [got0, got1, got2, got3])


def solution(mesh):
    return jax.shard_map(
        local,
        mesh=mesh,
        in_specs=(
            P(None, ("leaf", "panel"), None),
            P(None, ("leaf", "panel"), None),
            P(None, ("leaf", "panel"), None),
            P(None, ("leaf", "panel")),
            P(None, ("leaf", "panel")),
            P(None, ("leaf", "panel")),
            P(("leaf", "panel"), None),
            P(("leaf", "panel"), None),
            P(("leaf", "panel"), None),
        ),
        out_specs=P(None, ("leaf", "panel"), None),
        check_vma=False,
    )
```

```python
import jax
import jax.numpy as jnp
from jax import lax
from jax.experimental import pallas as pl
from jax.experimental.pallas import tpu as pltpu
from jax.sharding import PartitionSpec as P

LEVELS = 3
BLK = 128
NY = 4
NX = 4
HALF = 128
F32 = jnp.float32
BF16 = jnp.bfloat16
VMEM_LIMIT = 16 << 20

OFFSETS = ((1, 2), (0, 2), (1, 1), (1, 3), (0, 1), (0, 3), (1, 0))
OFFSETS_1 = OFFSETS[::-1]

CORE, ZBASE, VIDX, BLK1, KBLK1, BLK2, KBLK2 = 0, 1, 2, 6, 14, 22, 38
TABLE = 54


def route(shard, target):
    pairs = []
    for z in range(4):
        for y in range(NY):
            for x in range(NX):
                for c in range(2):
                    to = target(z, y, x, c)
                    if to is None:
                        continue
                    tz, ty, tx, tc = to
                    pairs.append(
                        (((z * NY + y) * NX + x) * 2 + c, ((tz * NY + ty) * NX + tx) * 2 + tc)
                    )
    return lax.ppermute(shard, ("leaf", "panel"), pairs)


def to_core(shard):
    return route(shard, lambda z, y, x, c: (z, y, x, 1 - c))


def to_z(shard):
    return route(shard, lambda z, y, x, c: (z ^ 1, y, x, c))


def shift_u(shard, r):
    return route(
        shard,
        lambda z, y, x, c: (z, y, (x + r) % NX, c) if c == 0 else (z, (y + r) % NY, x, c),
    )


def shift_v(shard, r):
    return route(
        shard,
        lambda z, y, x, c: (z, (y + r) % NY, x, c) if c == 0 else (z, y, (x + r) % NX, c),
    )


def near(shard, j):
    def target(z, y, x, c):
        dy, dx = OFFSETS[j] if c == 0 else OFFSETS_1[j]
        return (z, y ^ dy, (x + dx) % NX, c)

    return route(shard, target)


def split(a):
    high = a.astype(BF16)
    low = (a - high.astype(F32)).astype(BF16)
    return high, low


def paired(a):
    high, low = split(a)
    return jnp.concatenate([high, low], axis=1)


def mul(weights, pair):
    both = jnp.concatenate(split(weights), axis=1)
    twice = jnp.concatenate([pair, pair], axis=0)
    r = jnp.dot(both, twice, preferred_element_type=F32)
    return r[:, :HALF] + r[:, HALF:]


def exact(a, b):
    return mul(a, paired(b))


WHOLE = pl.BlockSpec(memory_space=pltpu.VMEM)
HBM = pl.BlockSpec(memory_space=pl.ANY)
SMEM = pl.BlockSpec(memory_space=pltpu.SMEM)
TILE = (BLK, HALF)
PAIR = (2, BLK, HALF)


def run(body, table, ins, outs, scratch=()):
    return pl.pallas_call(
        body,
        in_specs=[SMEM] + [spec for _, spec in ins],
        out_specs=[WHOLE] * len(outs),
        out_shape=[jax.ShapeDtypeStruct(s, F32) for s in outs],
        scratch_shapes=list(scratch),
        compiler_params=pltpu.CompilerParams(vmem_limit_bytes=VMEM_LIMIT),
    )(table, *[a for a, _ in ins])


def copy(src, dst, sem):
    cp = pltpu.make_async_copy(src, dst, sem)
    cp.start()
    return cp


SMALL_SCRATCH = [
    pltpu.VMEM(PAIR, F32),
    pltpu.VMEM(PAIR, F32),
    pltpu.SemaphoreType.DMA((4,)),
]


def small_start(level, c, rhs_refs, inv_refs, scratch):
    rbuf, mbuf, sems = scratch
    copies = []
    for i, r in enumerate(rhs_refs):
        lane = pl.multiple_of(c * HALF, HALF)
        copies.append(copy(r.at[level, :, pl.ds(lane, HALF)], rbuf.at[i], sems.at[i]))
    for i, r in enumerate(inv_refs):
        copies.append(copy(r.at[level], mbuf.at[i], sems.at[2 + i]))
    return copies


def wait_all(copies):
    for cp in copies:
        cp.wait()


def window_of(tab, block):
    return pl.ds(pl.multiple_of(start_of(tab, block), 2 * BLK), 2 * BLK)


def start_of(tab, block):
    place, half = block
    number = tab[place]
    if half:
        number = number + NY * NX * (tab[ZBASE] if half == 1 else 1 - tab[ZBASE])
    return number * (2 * BLK)


def forward_step(table, finish, extra_y, sources, blocks):
    flat = [b for g in blocks for b in g]
    nsrc = len(sources)
    ins = []
    npiece = 0
    if finish is not None:
        level, pieces, rhs, rhs_other, inv, inv_other = finish
        npiece = len(pieces)
        ins += [(p, WHOLE) for p in pieces]
        ins += [(a, HBM) for a in (rhs, rhs_other, inv, inv_other)]
    nfin = len(ins)
    ins += [(a, WHOLE) for a in extra_y]
    ny = len(ins)
    ins += [(a, WHOLE) for a in sources]
    nin = len(ins)
    outs = [PAIR] if finish is not None else []
    outs += [PAIR if len(g) == 1 else (len(g),) + PAIR for g in blocks]

    def body(tab, *refs):
        in_refs, out_refs = refs[:nin], list(refs[nin : nin + len(outs)])
        scratch = list(refs[nin + len(outs) :])
        c = tab[CORE]
        if finish is not None:
            small = scratch[-3:]
            rhs_refs, inv_refs = in_refs[npiece : npiece + 2], in_refs[npiece + 2 : nfin]
            smalls = small_start(level, c, rhs_refs, inv_refs, small)
        ys = []
        if finish is not None:
            y_ref = out_refs.pop(0)
            wait_all(smalls)
            for n, idx in enumerate((c, 1 - c)):
                t = small[0][n]
                if npiece:
                    update = in_refs[0][idx]
                    for p in in_refs[1:npiece]:
                        update = update + p[idx]
                    t = t - update
                y = exact(small[1][n], t)
                y_ref[idx] = y
                ys.append(y)
        if not flat:
            return
        for y_in in in_refs[nfin:ny]:
            ys += [y_in[c], y_in[1 - c]]
        pair = paired(jnp.concatenate(ys, axis=0))
        for g, out in zip(blocks, out_refs):
            rows = []
            for b in g:
                window = window_of(tab, b)
                rows.append(jnp.concatenate([w[window, :] for w in in_refs[ny:]], axis=1))
            r = mul(jnp.concatenate(rows, axis=0), pair)
            out[...] = r.reshape(out.shape)

    return run(body, table, ins, outs, SMALL_SCRATCH if finish is not None else [])


def sum_step(table, halves):
    sizes = [len(parts) for parts in halves]
    width = 4 // len(halves)

    def body(tab, *refs):
        out, buf = refs[-5:-1], refs[-1]
        at = 0
        for half, n in enumerate(sizes):
            total = refs[at][...]
            for p in refs[at + 1 : at + n]:
                total = total + p[...]
            buf[half * width : (half + 1) * width] = total
            at += n
        for vr in range(4):
            out[vr][...] = buf[tab[VIDX + vr]]

    ins = [(p, WHOLE) for parts in halves for p in parts]
    return run(body, table, ins, [PAIR] * 4, [pltpu.VMEM((4,) + PAIR, F32)])


def add_step(table, groups):
    n = sum(len(g) for g in groups)

    def body(tab, *refs):
        at = 0
        for i, g in enumerate(groups):
            total = refs[at][...]
            for p in refs[at + 1 : at + len(g)]:
                total = total + p[...]
            refs[n + i][...] = total
            at += len(g)

    ins = [(a, WHOLE) for g in groups for a in g]
    return run(body, table, ins, [g[0].shape for g in groups])


def pair_step(table, halves):
    sizes = [len(parts) for parts in halves]

    def body(tab, *refs):
        for vr in range(4):
            idx = tab[VIDX + vr]
            at = 0
            for half, n in enumerate(sizes):
                total = refs[at][idx]
                for p in refs[at + 1 : at + n]:
                    total = total + p[idx]
                refs[sum(sizes) + vr][half] = total
                at += n

    ins = [(p, WHOLE) for parts in halves for p in parts]
    return run(body, table, ins, [(2,) + PAIR] * 4)


def cross_step(table, pieces):
    n = len(pieces)

    def body(tab, *refs):
        for half in range(2):
            total = refs[0][half]
            for p in refs[1:n]:
                total = total + p[half]
            refs[n + half][...] = total

    return run(body, table, [(p, WHOLE) for p in pieces], [PAIR, PAIR])


def top_step(table, pieces, rhs, rhs_other, low, low_other, up, up_other):
    n = len(pieces)

    def body(tab, *refs):
        r0, r1, l0, l1, u0, u1, x_ref, mine_ref, send_ref = refs[n : n + 9]
        rbuf, mbuf, sems, ubuf, usems = refs[n + 9 :]
        c = tab[CORE]
        copies = small_start(LEVELS, c, (r0, r1), (l0, l1), (rbuf, mbuf, sems))
        for i, r in enumerate((u0, u1)):
            copies.append(copy(r.at[LEVELS], ubuf.at[i], usems.at[i]))
        wait_all(copies)
        for i, (idx, part) in enumerate(((c, mine_ref), (1 - c, send_ref))):
            update = refs[0][idx]
            for p in refs[1:n]:
                update = update + p[idx]
            x = exact(ubuf[i], exact(mbuf[i], rbuf[i] - update))
            x_ref[idx] = x
            part[...] = x

    ins = [(p, WHOLE) for p in pieces]
    ins += [(a, HBM) for a in (rhs, rhs_other, low, low_other, up, up_other)]
    scratch = SMALL_SCRATCH + [pltpu.VMEM(PAIR, F32), pltpu.SemaphoreType.DMA((2,))]
    return run(body, table, ins, [PAIR, TILE, TILE], scratch)


def backward_step(table, before, pieces, places, sources, finish):
    nsrc = len(sources)
    npiece = len(pieces)
    flat = [b for p in places for b in p]
    ins = [(p, WHOLE) for p in pieces]
    if before is not None:
        ins.append((before, WHOLE))
    nacc = len(ins)
    if finish is not None:
        level, y, inv, inv_other = finish
        ins += [(y, WHOLE), (inv, HBM), (inv_other, HBM)]
        outs = [PAIR, TILE, TILE]
    else:
        outs = [(nsrc * BLK, HALF)]
    nf = len(ins)
    ins += [(a, WHOLE) for a in sources]
    nin = len(ins)

    def body(tab, *refs):
        in_refs, out_refs = refs[:nin], refs[nin : nin + len(outs)]
        c = tab[CORE]
        if finish is not None:
            small = refs[nin + len(outs) :]
            smalls = small_start(level, c, (), in_refs[nacc + 1 : nf], small)
        rows = [p[...].reshape(-1, HALF) for p in in_refs[:npiece]]
        pair = paired(jnp.concatenate(rows, axis=0))
        wide = [
            jnp.concatenate([u[:, window_of(tab, b)] for u in in_refs[nf:]], axis=0)
            for b in flat
        ]
        high, low = split(jnp.concatenate(wide, axis=1))
        total = jnp.dot(high, pair, preferred_element_type=F32)
        total = total + jnp.dot(low, pair, preferred_element_type=F32)
        total = total[:, :HALF] + total[:, HALF:]
        if before is not None:
            total = total + in_refs[npiece][...]
        if finish is None:
            out_refs[0][...] = total
            return
        x_ref, mine_ref, send_ref = out_refs
        y_ref = in_refs[nacc]
        wait_all(smalls)
        for n, (idx, part) in enumerate(((c, mine_ref), (1 - c, send_ref))):
            x = exact(small[1][n], y_ref[idx] - total[n * BLK : (n + 1) * BLK])
            x_ref[idx] = x
            part[...] = x

    return run(body, table, ins, outs, SMALL_SCRATCH if finish is not None else [])


def assemble(table, mine, received):
    def body(tab, *refs):
        out = refs[8]
        for k in range(4):
            a, b = refs[k][...], refs[4 + k][...]
            first = tab[CORE] == 0
            out[k, :, :HALF] = jnp.where(first, a, b)
            out[k, :, HALF:] = jnp.where(first, b, a)

    ins = [(a, WHOLE) for a in mine + received]
    return run(body, table, ins, [(4, BLK, 2 * HALF)])[0]


def make_table(leaf, panel):
    z, y = leaf // NY, leaf % NY
    x, c = panel // 2, panel % 2
    u = jnp.where(c == 0, x, y)
    v = jnp.where(c == 0, y, x)
    four = jnp.arange(4, dtype=jnp.int32)
    ur, vr = jnp.repeat(four, 4), jnp.tile(four, 4)

    def offset(k):
        a = jnp.array([o[k] for o in OFFSETS] + [0], jnp.int32)
        b = jnp.array([o[k] for o in OFFSETS_1] + [0], jnp.int32)
        return jnp.where(c == 0, a, b)

    dy, dx = offset(0), offset(1)

    def plane(up, vp):
        return jnp.where(c == 0, vp * NX + up, up * NX + vp)

    parts = [
        jnp.stack([c, z % 2]),
        (v + four) % 4,
        ((y ^ dy) & 1) * NX + (x + dx) % NX,
        ((y ^ dy) & 1) * NX + (x - dx + NX) % NX,
        plane((u + ur) % 4, vr),
        plane((u - ur + 4) % 4, (v - vr + 4) % 4),
    ]
    return jnp.concatenate([p.astype(jnp.int32) for p in parts])


def after(value, other):
    return lax.optimization_barrier((value, other))[0]


def local(
    rhs,
    lower_inv,
    upper_inv,
    lower_coupling_1,
    lower_coupling_2,
    lower_coupling_3,
    upper_coupling_1,
    upper_coupling_2,
    upper_coupling_3,
):
    leaf, panel = lax.axis_index("leaf"), lax.axis_index("panel")
    table = make_table(leaf, panel)

    rhs_o = to_core(rhs)
    low_o = to_core(lower_inv)
    l1_o = to_core(lower_coupling_1)
    lows = (rhs, rhs_o, lower_inv, low_o)
    y0, *parts = forward_step(
        table,
        (0, []) + lows,
        [],
        [lower_coupling_1, l1_o],
        [[(BLK1 + j, 0)] for j in range(8)],
    )
    l2_o = to_core(after(lower_coupling_2, y0))
    pieces = [parts[7]] + [near(parts[j], j) for j in range(7)]

    def across(halves):
        own, *sends = sum_step(table, halves)
        return [own] + [shift_v(p, r) for r, p in zip((1, 2, 3), sends)]

    def across_z(halves):
        pieces = pair_step(table, halves)
        pieces = [pieces[0]] + [shift_v(p, r) for r, p in zip((1, 2, 3), pieces[1:])]
        own, other = cross_step(table, pieces)
        return [own, to_z(other)]

    def spread(finish, ys, sources, first, second):
        out = forward_step(table, finish, ys, sources, [first[2], second[2]])
        a2, b2 = shift_u(out[-2], 1), shift_u(out[-1], -1)
        if finish is not None:
            ys = [out[0]]
        d1, d3 = forward_step(table, None, ys, sources, [second[1], first[3]])
        d1, d3 = shift_u(d1, 1), shift_u(d3, -1)
        s1, s3 = forward_step(table, None, ys, sources, [first[1], second[3]])
        s1, s3 = add_step(table, [(s1, a2), (s3, b2)])
        s1, s3 = shift_u(s1, 1), shift_u(s3, -1)
        a0, b0 = forward_step(table, None, ys, sources, [first[0], second[0]])
        halves = [[a0, d3, s1], [b0, d1, s3]]
        return ys[0], across(halves) if a0.shape[0] == 2 else across_z(halves)

    def half_plane(base, columns, z):
        return [[(base + ur * 4 + v, z) for v in columns] for ur in range(4)]

    y1, pieces = spread(
        (1, pieces) + lows,
        [],
        [lower_coupling_2, l2_o],
        half_plane(BLK2, (0, 1), 0),
        half_plane(BLK2, (2, 3), 0),
    )
    l3_o = to_core(after(lower_coupling_3, y1))
    up_o = to_core(after(upper_inv, y1))
    y2, pieces = spread(
        (2, pieces) + lows,
        [],
        [lower_coupling_3, l3_o],
        half_plane(BLK2, range(4), 1),
        half_plane(BLK2, range(4), 2),
    )
    u3_o = to_core(after(upper_coupling_3, y2))
    x3, mine3, send3 = top_step(table, pieces, *lows, upper_inv, up_o)
    got3 = to_core(send3)
    u2_o = to_core(after(upper_coupling_2, x3))

    def along_v(x):
        return [x] + [shift_v(x, r) for r in (1, 2, 3)]

    def around(a, b):
        a1, b3 = shift_u(a, 1), shift_u(b, -1)
        b1, a3 = shift_u(b, 1), shift_u(a, -1)
        a2, b2 = shift_u(a1, 1), shift_u(b3, -1)
        return [(a, b), (a1, b1), (a2, b2), (a3, b3)]

    def gathered(rings, first, second, sources, finish):
        acc = None
        for urs, last in (((0,), None), ((1, 3), None), ((2,), finish)):
            arrays, places = [], []
            for ur in urs:
                arrays += rings[ur]
                places += [first[ur], second[ur]]
            out = backward_step(table, acc, arrays, places, sources, last)
            acc = out[0]
        return out

    line = jnp.stack(along_v(x3))
    x2, mine2, send2 = gathered(
        around(line, to_z(line)),
        half_plane(KBLK2, range(4), 1),
        half_plane(KBLK2, range(4), 2),
        [upper_coupling_3, u3_o],
        (2, y2, upper_inv, up_o),
    )
    got2 = to_core(send2)
    u1_o = to_core(after(upper_coupling_1, x2))
    line = along_v(x2)
    rings = around(jnp.stack(line[:2]), jnp.stack(line[2:]))
    x1, mine1, send1 = gathered(
        rings,
        half_plane(KBLK2, (0, 1), 0),
        half_plane(KBLK2, (2, 3), 0),
        [upper_coupling_2, u2_o],
        (1, y1, upper_inv, up_o),
    )
    got1 = to_core(send1)

    sources = [upper_coupling_1, u1_o]
    arrivals = [near(x1, j) for j in range(7)]
    places = [[(KBLK1 + j, 0)] for j in range(8)]
    (acc,) = backward_step(table, None, [x1], places[7:], sources, None)
    (acc,) = backward_step(table, acc, arrivals[:4], places[:4], sources, None)
    _, mine0, send0 = backward_step(
        table, acc, arrivals[4:], places[4:7], sources, (0, y0, upper_inv, up_o)
    )
    got0 = to_core(send0)
    return assemble(table, [mine0, mine1, mine2, mine3], [got0, got1, got2, got3])


def solution(mesh):
    return jax.shard_map(
        local,
        mesh=mesh,
        in_specs=(
            P(None, ("leaf", "panel"), None),
            P(None, ("leaf", "panel"), None),
            P(None, ("leaf", "panel"), None),
            P(None, ("leaf", "panel")),
            P(None, ("leaf", "panel")),
            P(None, ("leaf", "panel")),
            P(("leaf", "panel"), None),
            P(("leaf", "panel"), None),
            P(("leaf", "panel"), None),
        ),
        out_specs=P(None, ("leaf", "panel"), None),
        check_vma=False,
    )
```

```python
import jax
import jax.numpy as jnp
from jax import lax
from jax.experimental import pallas as pl
from jax.experimental.pallas import tpu as pltpu
from jax.sharding import PartitionSpec as P

LEVELS = 3
BLK = 128
NY = 4
NX = 4
HALF = 128
F32 = jnp.float32
BF16 = jnp.bfloat16
VMEM_LIMIT = 16 << 20

OFFSETS = ((1, 2), (0, 2), (1, 1), (1, 3), (0, 1), (0, 3), (1, 0))
OFFSETS_1 = OFFSETS[::-1]
OUTWARD = ((0, 1), (0, 3), (1, 0), (1, 1), (1, 3), (0, 2), (1, 2))
OUTWARD_1 = ((1, 0), (0, 1), (0, 3), (0, 2), (1, 2), (1, 1), (1, 3))

CORE, ZBASE, VIDX, BLK1, KBLK1, BLK2, KBLK2 = 0, 1, 2, 6, 14, 22, 38
TABLE = 54


def route(shard, target):
    pairs = []
    for z in range(4):
        for y in range(NY):
            for x in range(NX):
                for c in range(2):
                    to = target(z, y, x, c)
                    if to is None:
                        continue
                    tz, ty, tx, tc = to
                    pairs.append(
                        (((z * NY + y) * NX + x) * 2 + c, ((tz * NY + ty) * NX + tx) * 2 + tc)
                    )
    return lax.ppermute(shard, ("leaf", "panel"), pairs)


def to_core(shard):
    return route(shard, lambda z, y, x, c: (z, y, x, 1 - c))


def to_z(shard):
    return route(shard, lambda z, y, x, c: (z ^ 1, y, x, c))


def shift_u(shard, r):
    return route(
        shard,
        lambda z, y, x, c: (z, y, (x + r) % NX, c) if c == 0 else (z, (y + r) % NY, x, c),
    )


def shift_v(shard, r):
    return route(
        shard,
        lambda z, y, x, c: (z, (y + r) % NY, x, c) if c == 0 else (z, y, (x + r) % NX, c),
    )


def near(shard, orders, j):
    def target(z, y, x, c):
        dy, dx = orders[c][j]
        return (z, y ^ dy, (x + dx) % NX, c)

    return route(shard, target)


def split(a):
    high = a.astype(BF16)
    low = (a - high.astype(F32)).astype(BF16)
    return high, low


def paired(a):
    high, low = split(a)
    return jnp.concatenate([high, low], axis=1)


def mul(weights, pair):
    both = jnp.concatenate(split(weights), axis=1)
    twice = jnp.concatenate([pair, pair], axis=0)
    r = jnp.dot(both, twice, preferred_element_type=F32)
    return r[:, :HALF] + r[:, HALF:]


def exact(a, b):
    return mul(a, paired(b))


WHOLE = pl.BlockSpec(memory_space=pltpu.VMEM)
HBM = pl.BlockSpec(memory_space=pl.ANY)
SMEM = pl.BlockSpec(memory_space=pltpu.SMEM)
TILE = (BLK, HALF)
PAIR = (2, BLK, HALF)


def run(body, table, ins, outs, scratch=()):
    return pl.pallas_call(
        body,
        in_specs=[SMEM] + [spec for _, spec in ins],
        out_specs=[WHOLE] * len(outs),
        out_shape=[jax.ShapeDtypeStruct(s, F32) for s in outs],
        scratch_shapes=list(scratch),
        compiler_params=pltpu.CompilerParams(vmem_limit_bytes=VMEM_LIMIT),
    )(table, *[a for a, _ in ins])


def copy(src, dst, sem):
    cp = pltpu.make_async_copy(src, dst, sem)
    cp.start()
    return cp


SMALL_SCRATCH = [
    pltpu.VMEM(PAIR, F32),
    pltpu.VMEM(PAIR, F32),
    pltpu.SemaphoreType.DMA((4,)),
]


def small_start(level, c, rhs_refs, inv_refs, scratch):
    rbuf, mbuf, sems = scratch
    copies = []
    for i, r in enumerate(rhs_refs):
        lane = pl.multiple_of(c * HALF, HALF)
        copies.append(copy(r.at[level, :, pl.ds(lane, HALF)], rbuf.at[i], sems.at[i]))
    for i, r in enumerate(inv_refs):
        copies.append(copy(r.at[level], mbuf.at[i], sems.at[2 + i]))
    return copies


def wait_all(copies):
    for cp in copies:
        cp.wait()


def window_of(tab, block):
    return pl.ds(pl.multiple_of(start_of(tab, block), 2 * BLK), 2 * BLK)


def start_of(tab, block):
    place, half = block
    number = tab[place]
    if half:
        number = number + NY * NX * (tab[ZBASE] if half == 1 else 1 - tab[ZBASE])
    return number * (2 * BLK)


def forward_step(table, finish, extra_y, sources, blocks):
    flat = [b for g in blocks for b in g]
    nsrc = len(sources)
    ins = []
    npiece = 0
    if finish is not None:
        level, pieces, rhs, rhs_other, inv, inv_other = finish
        npiece = len(pieces)
        ins += [(p, WHOLE) for p in pieces]
        ins += [(a, HBM) for a in (rhs, rhs_other, inv, inv_other)]
    nfin = len(ins)
    ins += [(a, WHOLE) for a in extra_y]
    ny = len(ins)
    ins += [(a, WHOLE) for a in sources]
    nin = len(ins)
    outs = [PAIR] if finish is not None else []
    outs += [PAIR if len(g) == 1 else (len(g),) + PAIR for g in blocks]

    def body(tab, *refs):
        in_refs, out_refs = refs[:nin], list(refs[nin : nin + len(outs)])
        scratch = list(refs[nin + len(outs) :])
        c = tab[CORE]
        if finish is not None:
            small = scratch[-3:]
            rhs_refs, inv_refs = in_refs[npiece : npiece + 2], in_refs[npiece + 2 : nfin]
            smalls = small_start(level, c, rhs_refs, inv_refs, small)
        ys = []
        if finish is not None:
            y_ref = out_refs.pop(0)
            wait_all(smalls)
            for n, idx in enumerate((c, 1 - c)):
                t = small[0][n]
                if npiece:
                    update = in_refs[0][idx]
                    for p in in_refs[1:npiece]:
                        update = update + p[idx]
                    t = t - update
                y = exact(small[1][n], t)
                y_ref[idx] = y
                ys.append(y)
        if not flat:
            return
        for y_in in in_refs[nfin:ny]:
            ys += [y_in[c], y_in[1 - c]]
        pair = paired(jnp.concatenate(ys, axis=0))
        for g, out in zip(blocks, out_refs):
            rows = []
            for b in g:
                window = window_of(tab, b)
                rows.append(jnp.concatenate([w[window, :] for w in in_refs[ny:]], axis=1))
            r = mul(jnp.concatenate(rows, axis=0), pair)
            out[...] = r.reshape(out.shape)

    return run(body, table, ins, outs, SMALL_SCRATCH if finish is not None else [])


def sum_step(table, halves):
    sizes = [len(parts) for parts in halves]
    width = 4 // len(halves)

    def body(tab, *refs):
        out, buf = refs[-5:-1], refs[-1]
        at = 0
        for half, n in enumerate(sizes):
            total = refs[at][...]
            for p in refs[at + 1 : at + n]:
                total = total + p[...]
            buf[half * width : (half + 1) * width] = total
            at += n
        for vr in range(4):
            out[vr][...] = buf[tab[VIDX + vr]]

    ins = [(p, WHOLE) for parts in halves for p in parts]
    return run(body, table, ins, [PAIR] * 4, [pltpu.VMEM((4,) + PAIR, F32)])


def add_step(table, groups):
    n = sum(len(g) for g in groups)

    def body(tab, *refs):
        at = 0
        for i, g in enumerate(groups):
            total = refs[at][...]
            for p in refs[at + 1 : at + len(g)]:
                total = total + p[...]
            refs[n + i][...] = total
            at += len(g)

    ins = [(a, WHOLE) for g in groups for a in g]
    return run(body, table, ins, [g[0].shape for g in groups])


def pair_step(table, halves):
    sizes = [len(parts) for parts in halves]

    def body(tab, *refs):
        for vr in range(4):
            idx = tab[VIDX + vr]
            at = 0
            for half, n in enumerate(sizes):
                total = refs[at][idx]
                for p in refs[at + 1 : at + n]:
                    total = total + p[idx]
                refs[sum(sizes) + vr][half] = total
                at += n

    ins = [(p, WHOLE) for parts in halves for p in parts]
    return run(body, table, ins, [(2,) + PAIR] * 4)


def cross_step(table, pieces):
    n = len(pieces)

    def body(tab, *refs):
        for half in range(2):
            total = refs[0][half]
            for p in refs[1:n]:
                total = total + p[half]
            refs[n + half][...] = total

    return run(body, table, [(p, WHOLE) for p in pieces], [PAIR, PAIR])


def top_step(table, pieces, rhs, rhs_other, low, low_other, up, up_other):
    n = len(pieces)

    def body(tab, *refs):
        r0, r1, l0, l1, u0, u1, x_ref, mine_ref, send_ref = refs[n : n + 9]
        rbuf, mbuf, sems, ubuf, usems = refs[n + 9 :]
        c = tab[CORE]
        copies = small_start(LEVELS, c, (r0, r1), (l0, l1), (rbuf, mbuf, sems))
        for i, r in enumerate((u0, u1)):
            copies.append(copy(r.at[LEVELS], ubuf.at[i], usems.at[i]))
        wait_all(copies)
        for i, (idx, part) in enumerate(((c, mine_ref), (1 - c, send_ref))):
            update = refs[0][idx]
            for p in refs[1:n]:
                update = update + p[idx]
            x = exact(ubuf[i], exact(mbuf[i], rbuf[i] - update))
            x_ref[idx] = x
            part[...] = x

    ins = [(p, WHOLE) for p in pieces]
    ins += [(a, HBM) for a in (rhs, rhs_other, low, low_other, up, up_other)]
    scratch = SMALL_SCRATCH + [pltpu.VMEM(PAIR, F32), pltpu.SemaphoreType.DMA((2,))]
    return run(body, table, ins, [PAIR, TILE, TILE], scratch)


def backward_step(table, before, pieces, places, sources, finish):
    nsrc = len(sources)
    npiece = len(pieces)
    flat = [b for p in places for b in p]
    ins = [(p, WHOLE) for p in pieces]
    if before is not None:
        ins.append((before, WHOLE))
    nacc = len(ins)
    if finish is not None:
        level, y, inv, inv_other = finish
        ins += [(y, WHOLE), (inv, HBM), (inv_other, HBM)]
        outs = [PAIR, TILE, TILE]
    else:
        outs = [(nsrc * BLK, HALF)]
    nf = len(ins)
    ins += [(a, WHOLE) for a in sources]
    nin = len(ins)

    def body(tab, *refs):
        in_refs, out_refs = refs[:nin], refs[nin : nin + len(outs)]
        c = tab[CORE]
        if finish is not None:
            small = refs[nin + len(outs) :]
            smalls = small_start(level, c, (), in_refs[nacc + 1 : nf], small)
        rows = [p[...].reshape(-1, HALF) for p in in_refs[:npiece]]
        pair = paired(jnp.concatenate(rows, axis=0))
        wide = [
            jnp.concatenate([u[:, window_of(tab, b)] for u in in_refs[nf:]], axis=0)
            for b in flat
        ]
        high, low = split(jnp.concatenate(wide, axis=1))
        total = jnp.dot(high, pair, preferred_element_type=F32)
        total = total + jnp.dot(low, pair, preferred_element_type=F32)
        total = total[:, :HALF] + total[:, HALF:]
        if before is not None:
            total = total + in_refs[npiece][...]
        if finish is None:
            out_refs[0][...] = total
            return
        x_ref, mine_ref, send_ref = out_refs
        y_ref = in_refs[nacc]
        wait_all(smalls)
        for n, (idx, part) in enumerate(((c, mine_ref), (1 - c, send_ref))):
            x = exact(small[1][n], y_ref[idx] - total[n * BLK : (n + 1) * BLK])
            x_ref[idx] = x
            part[...] = x

    return run(body, table, ins, outs, SMALL_SCRATCH if finish is not None else [])


def assemble(table, mine, received):
    def body(tab, *refs):
        out = refs[8]
        for k in range(4):
            a, b = refs[k][...], refs[4 + k][...]
            first = tab[CORE] == 0
            out[k, :, :HALF] = jnp.where(first, a, b)
            out[k, :, HALF:] = jnp.where(first, b, a)

    ins = [(a, WHOLE) for a in mine + received]
    return run(body, table, ins, [(4, BLK, 2 * HALF)])[0]


def make_table(leaf, panel):
    z, y = leaf // NY, leaf % NY
    x, c = panel // 2, panel % 2
    u = jnp.where(c == 0, x, y)
    v = jnp.where(c == 0, y, x)
    four = jnp.arange(4, dtype=jnp.int32)
    ur, vr = jnp.repeat(four, 4), jnp.tile(four, 4)

    def offset(orders, k):
        a = jnp.array([o[k] for o in orders[0]] + [0], jnp.int32)
        b = jnp.array([o[k] for o in orders[1]] + [0], jnp.int32)
        return jnp.where(c == 0, a, b)

    dy, dx = [offset((OUTWARD, OUTWARD_1), k) for k in (0, 1)]
    ey, ex = [offset((OFFSETS, OFFSETS_1), k) for k in (0, 1)]

    def plane(up, vp):
        return jnp.where(c == 0, vp * NX + up, up * NX + vp)

    parts = [
        jnp.stack([c, z % 2]),
        (v + four) % 4,
        ((y ^ dy) & 1) * NX + (x + dx) % NX,
        ((y ^ ey) & 1) * NX + (x - ex + NX) % NX,
        plane((u + ur) % 4, vr),
        plane((u - ur + 4) % 4, (v - vr + 4) % 4),
    ]
    return jnp.concatenate([p.astype(jnp.int32) for p in parts])


def after(value, other):
    return lax.optimization_barrier((value, other))[0]


def local(
    rhs,
    lower_inv,
    upper_inv,
    lower_coupling_1,
    lower_coupling_2,
    lower_coupling_3,
    upper_coupling_1,
    upper_coupling_2,
    upper_coupling_3,
):
    leaf, panel = lax.axis_index("leaf"), lax.axis_index("panel")
    table = make_table(leaf, panel)

    def held(a):
        return jnp.where(panel >= 0, a, 0.0)

    rhs_o = to_core(rhs)
    low_o = to_core(lower_inv)
    l1_o = to_core(lower_coupling_1)
    lows = (held(rhs), rhs_o, held(lower_inv), low_o)
    y0, *parts = forward_step(
        table,
        (0, []) + lows,
        [],
        [lower_coupling_1, l1_o],
        [[(BLK1 + j, 0)] for j in range(8)],
    )
    l2_o = to_core(after(lower_coupling_2, y0))
    pieces = [parts[7]] + [near(parts[j], (OUTWARD, OUTWARD_1), j) for j in range(7)]

    def along_v(pieces):
        got = {r: shift_v(pieces[r], r) for r in (2, 3, 1)}
        return [pieces[0], got[1], got[2], got[3]]

    def across(halves):
        return along_v(sum_step(table, halves))

    def across_z(halves):
        pieces = along_v(pair_step(table, halves))
        own, other = cross_step(table, pieces)
        return [own, to_z(other)]

    def spread(finish, ys, sources, first, second):
        out = forward_step(table, finish, ys, sources, [first[2], second[2]])
        a2, b2 = shift_u(out[-2], 1), shift_u(out[-1], -1)
        if finish is not None:
            ys = [out[0]]
        d1, d3 = forward_step(table, None, ys, sources, [second[1], first[3]])
        d1, d3 = shift_u(d1, 1), shift_u(d3, -1)
        s1, s3 = forward_step(table, None, ys, sources, [first[1], second[3]])
        s1, s3 = add_step(table, [(s1, a2), (s3, b2)])
        s1, s3 = shift_u(s1, 1), shift_u(s3, -1)
        a0, b0 = forward_step(table, None, ys, sources, [first[0], second[0]])
        halves = [[a0, d3, s1], [b0, d1, s3]]
        return ys[0], across(halves) if a0.shape[0] == 2 else across_z(halves)

    def half_plane(base, columns, z):
        return [[(base + ur * 4 + v, z) for v in columns] for ur in range(4)]

    y1, pieces = spread(
        (1, pieces) + lows,
        [],
        [lower_coupling_2, l2_o],
        half_plane(BLK2, (0, 1), 0),
        half_plane(BLK2, (2, 3), 0),
    )
    l3_o = to_core(after(lower_coupling_3, y1))
    up_o = to_core(after(upper_inv, y1))
    y2, pieces = spread(
        (2, pieces) + lows,
        [],
        [lower_coupling_3, l3_o],
        half_plane(BLK2, range(4), 1),
        half_plane(BLK2, range(4), 2),
    )
    u3_o = to_core(after(upper_coupling_3, y2))
    x3, mine3, send3 = top_step(table, pieces, *lows, upper_inv, up_o)
    got3 = to_core(send3)
    u2_o = to_core(after(upper_coupling_2, x3))

    def around_halves(a, b):
        a1, a3 = shift_u(a, 1), shift_u(a, -1)
        b1, b3 = shift_u(b, 1), shift_u(b, -1)
        return [a, a1, shift_u(a1, 1), a3], [b, b1, shift_u(b3, -1), b3]

    def gathered(groups, sources, finish):
        acc = None
        for i, group in enumerate(groups):
            last = finish if i == len(groups) - 1 else None
            arrays, places = zip(*group)
            out = backward_step(table, acc, arrays, places, sources, last)
            acc = out[0]
        return out

    line = jnp.stack(along_v([x3] * 4))
    own, other = around_halves(line, to_z(line))
    own = list(zip(own, half_plane(KBLK2, range(4), 1)))
    other = list(zip(other, half_plane(KBLK2, range(4), 2)))
    x2, mine2, send2 = gathered(
        [[g[0] for g in (own, other)], own[1::2] + other[1::2], own[2:3] + other[2:3]],
        [upper_coupling_3, u3_o],
        (2, y2, upper_inv, up_o),
    )
    got2 = to_core(send2)
    u1_o = to_core(after(upper_coupling_1, x2))
    line = along_v([x2] * 4)
    near_v, far_v = around_halves(jnp.stack(line[:2]), jnp.stack(line[2:]))
    near_v = list(zip(near_v, half_plane(KBLK2, (0, 1), 0)))
    far_v = list(zip(far_v, half_plane(KBLK2, (2, 3), 0)))
    x1, mine1, send1 = gathered(
        [near_v[:1] + far_v[:1], near_v[1::2] + far_v[1::2], near_v[2:3] + far_v[2:3]],
        [upper_coupling_2, u2_o],
        (1, y1, upper_inv, up_o),
    )
    got1 = to_core(send1)

    sources = [upper_coupling_1, u1_o]
    arrivals = [near(x1, (OFFSETS, OFFSETS_1), j) for j in range(7)]
    places = [[(KBLK1 + j, 0)] for j in range(8)]
    (acc,) = backward_step(table, None, [x1], places[7:], sources, None)
    (acc,) = backward_step(table, acc, arrivals[:4], places[:4], sources, None)
    _, mine0, send0 = backward_step(
        table, acc, arrivals[4:], places[4:7], sources, (0, y0, upper_inv, up_o)
    )
    got0 = to_core(send0)
    return assemble(table, [mine0, mine1, mine2, mine3], [got0, got1, got2, got3])


def solution(mesh):
    return jax.shard_map(
        local,
        mesh=mesh,
        in_specs=(
            P(None, ("leaf", "panel"), None),
            P(None, ("leaf", "panel"), None),
            P(None, ("leaf", "panel"), None),
            P(None, ("leaf", "panel")),
            P(None, ("leaf", "panel")),
            P(None, ("leaf", "panel")),
            P(("leaf", "panel"), None),
            P(("leaf", "panel"), None),
            P(("leaf", "panel"), None),
        ),
        out_specs=P(None, ("leaf", "panel"), None),
        check_vma=False,
    )
```

```python
import jax
import jax.numpy as jnp
from jax import lax
from jax.experimental import pallas as pl
from jax.experimental.pallas import tpu as pltpu
from jax.sharding import PartitionSpec as P

LEVELS = 3
BLK = 128
NY = 4
NX = 4
HALF = 128
F32 = jnp.float32
BF16 = jnp.bfloat16
VMEM_LIMIT = 16 << 20

OFFSETS = ((1, 2), (0, 2), (1, 1), (1, 3), (0, 1), (0, 3), (1, 0))
OFFSETS_1 = OFFSETS[::-1]
OUTWARD = ((0, 1), (0, 3), (1, 0), (1, 1), (1, 3), (0, 2), (1, 2))
OUTWARD_1 = ((1, 0), (0, 1), (0, 3), (0, 2), (1, 2), (1, 1), (1, 3))

CORE, ZBASE, VIDX, BLK1, KBLK1, BLK2, KBLK2 = 0, 1, 2, 6, 14, 22, 38
TABLE = 54


def route(shard, target):
    pairs = []
    for z in range(4):
        for y in range(NY):
            for x in range(NX):
                for c in range(2):
                    to = target(z, y, x, c)
                    if to is None:
                        continue
                    tz, ty, tx, tc = to
                    pairs.append(
                        (((z * NY + y) * NX + x) * 2 + c, ((tz * NY + ty) * NX + tx) * 2 + tc)
                    )
    return lax.ppermute(shard, ("leaf", "panel"), pairs)


def to_core(shard):
    return route(shard, lambda z, y, x, c: (z, y, x, 1 - c))


def to_z(shard):
    return route(shard, lambda z, y, x, c: (z ^ 1, y, x, c))


def shift_u(shard, r):
    return route(
        shard,
        lambda z, y, x, c: (z, y, (x + r) % NX, c) if c == 0 else (z, (y + r) % NY, x, c),
    )


def shift_v(shard, r):
    return route(
        shard,
        lambda z, y, x, c: (z, (y + r) % NY, x, c) if c == 0 else (z, y, (x + r) % NX, c),
    )


def near(shard, orders, j):
    def target(z, y, x, c):
        dy, dx = orders[c][j]
        return (z, y ^ dy, (x + dx) % NX, c)

    return route(shard, target)


def split(a):
    high = a.astype(BF16)
    low = (a - high.astype(F32)).astype(BF16)
    return high, low


def paired(a):
    high, low = split(a)
    return jnp.concatenate([high, low], axis=1)


def mul(weights, pair):
    both = jnp.concatenate(split(weights), axis=1)
    twice = jnp.concatenate([pair, pair], axis=0)
    r = jnp.dot(both, twice, preferred_element_type=F32)
    return r[:, :HALF] + r[:, HALF:]


def exact(a, b):
    return mul(a, paired(b))


WHOLE = pl.BlockSpec(memory_space=pltpu.VMEM)
HBM = pl.BlockSpec(memory_space=pl.ANY)
SMEM = pl.BlockSpec(memory_space=pltpu.SMEM)
TILE = (BLK, HALF)
PAIR = (2, BLK, HALF)


def run(body, table, ins, outs, scratch=()):
    return pl.pallas_call(
        body,
        in_specs=[SMEM] + [spec for _, spec in ins],
        out_specs=[WHOLE] * len(outs),
        out_shape=[jax.ShapeDtypeStruct(s, F32) for s in outs],
        scratch_shapes=list(scratch),
        compiler_params=pltpu.CompilerParams(vmem_limit_bytes=VMEM_LIMIT),
    )(table, *[a for a, _ in ins])


def copy(src, dst, sem):
    cp = pltpu.make_async_copy(src, dst, sem)
    cp.start()
    return cp


SMALL_SCRATCH = [
    pltpu.VMEM(PAIR, F32),
    pltpu.VMEM(PAIR, F32),
    pltpu.SemaphoreType.DMA((4,)),
]


def small_start(level, c, rhs_refs, inv_refs, scratch):
    rbuf, mbuf, sems = scratch
    copies = []
    for i, r in enumerate(rhs_refs):
        lane = pl.multiple_of(c * HALF, HALF)
        copies.append(copy(r.at[level, :, pl.ds(lane, HALF)], rbuf.at[i], sems.at[i]))
    for i, r in enumerate(inv_refs):
        copies.append(copy(r.at[level], mbuf.at[i], sems.at[2 + i]))
    return copies


def wait_all(copies):
    for cp in copies:
        cp.wait()


def window_of(tab, block):
    return pl.ds(pl.multiple_of(start_of(tab, block), 2 * BLK), 2 * BLK)


def start_of(tab, block):
    place, half = block
    number = tab[place]
    if half:
        number = number + NY * NX * (tab[ZBASE] if half == 1 else 1 - tab[ZBASE])
    return number * (2 * BLK)


def forward_step(table, finish, extra_y, sources, blocks):
    flat = [b for g in blocks for b in g]
    nsrc = len(sources)
    ins = []
    npiece = 0
    if finish is not None:
        level, pieces, rhs, rhs_other, inv, inv_other = finish
        npiece = len(pieces)
        ins += [(p, WHOLE) for p in pieces]
        ins += [(a, HBM) for a in (rhs, rhs_other, inv, inv_other)]
    nfin = len(ins)
    ins += [(a, WHOLE) for a in extra_y]
    ny = len(ins)
    ins += [(a, WHOLE) for a in sources]
    nin = len(ins)
    outs = [PAIR] if finish is not None else []
    outs += [PAIR if len(g) == 1 else (len(g),) + PAIR for g in blocks]

    def body(tab, *refs):
        in_refs, out_refs = refs[:nin], list(refs[nin : nin + len(outs)])
        scratch = list(refs[nin + len(outs) :])
        c = tab[CORE]
        if finish is not None:
            small = scratch[-3:]
            rhs_refs, inv_refs = in_refs[npiece : npiece + 2], in_refs[npiece + 2 : nfin]
            smalls = small_start(level, c, rhs_refs, inv_refs, small)
        ys = []
        if finish is not None:
            y_ref = out_refs.pop(0)
            wait_all(smalls)
            for n, idx in enumerate((c, 1 - c)):
                t = small[0][n]
                if npiece:
                    update = in_refs[0][idx]
                    for p in in_refs[1:npiece]:
                        update = update + p[idx]
                    t = t - update
                y = exact(small[1][n], t)
                y_ref[idx] = y
                ys.append(y)
        if not flat:
            return
        for y_in in in_refs[nfin:ny]:
            ys += [y_in[c], y_in[1 - c]]
        pair = paired(jnp.concatenate(ys, axis=0))
        for g, out in zip(blocks, out_refs):
            rows = []
            for b in g:
                window = window_of(tab, b)
                rows.append(jnp.concatenate([w[window, :] for w in in_refs[ny:]], axis=1))
            r = mul(jnp.concatenate(rows, axis=0), pair)
            out[...] = r.reshape(out.shape)

    return run(body, table, ins, outs, SMALL_SCRATCH if finish is not None else [])


def sum_step(table, halves):
    sizes = [len(parts) for parts in halves]
    width = 4 // len(halves)

    def body(tab, *refs):
        out, buf = refs[-5:-1], refs[-1]
        at = 0
        for half, n in enumerate(sizes):
            total = refs[at][...]
            for p in refs[at + 1 : at + n]:
                total = total + p[...]
            buf[half * width : (half + 1) * width] = total
            at += n
        for vr in range(4):
            out[vr][...] = buf[tab[VIDX + vr]]

    ins = [(p, WHOLE) for parts in halves for p in parts]
    return run(body, table, ins, [PAIR] * 4, [pltpu.VMEM((4,) + PAIR, F32)])


def add_step(table, groups):
    n = sum(len(g) for g in groups)

    def body(tab, *refs):
        at = 0
        for i, g in enumerate(groups):
            total = refs[at][...]
            for p in refs[at + 1 : at + len(g)]:
                total = total + p[...]
            refs[n + i][...] = total
            at += len(g)

    ins = [(a, WHOLE) for g in groups for a in g]
    return run(body, table, ins, [g[0].shape for g in groups])


def pair_step(table, halves):
    sizes = [len(parts) for parts in halves]

    def body(tab, *refs):
        for vr in range(4):
            idx = tab[VIDX + vr]
            at = 0
            for half, n in enumerate(sizes):
                total = refs[at][idx]
                for p in refs[at + 1 : at + n]:
                    total = total + p[idx]
                refs[sum(sizes) + vr][half] = total
                at += n

    ins = [(p, WHOLE) for parts in halves for p in parts]
    return run(body, table, ins, [(2,) + PAIR] * 4)


def cross_step(table, pieces):
    n = len(pieces)

    def body(tab, *refs):
        total = refs[0][1]
        for p in refs[1:n]:
            total = total + p[1]
        refs[n][...] = total

    return run(body, table, [(p, WHOLE) for p in pieces], [PAIR])[0]


def top_step(table, pieces, rhs, rhs_other, low, low_other, up, up_other):
    n = len(pieces)

    def body(tab, *refs):
        r0, r1, l0, l1, u0, u1, x_ref, mine_ref, send_ref = refs[n : n + 9]
        rbuf, mbuf, sems, ubuf, usems = refs[n + 9 :]
        c = tab[CORE]
        copies = small_start(LEVELS, c, (r0, r1), (l0, l1), (rbuf, mbuf, sems))
        for i, r in enumerate((u0, u1)):
            copies.append(copy(r.at[LEVELS], ubuf.at[i], usems.at[i]))
        wait_all(copies)
        for i, (idx, part) in enumerate(((c, mine_ref), (1 - c, send_ref))):
            update = refs[0][idx]
            for p in refs[1:n]:
                update = update + p[0, idx]
            x = exact(ubuf[i], exact(mbuf[i], rbuf[i] - update))
            x_ref[idx] = x
            part[...] = x

    ins = [(p, WHOLE) for p in pieces]
    ins += [(a, HBM) for a in (rhs, rhs_other, low, low_other, up, up_other)]
    scratch = SMALL_SCRATCH + [pltpu.VMEM(PAIR, F32), pltpu.SemaphoreType.DMA((2,))]
    return run(body, table, ins, [PAIR, TILE, TILE], scratch)


def backward_step(table, before, pieces, places, sources, finish):
    nsrc = len(sources)
    npiece = len(pieces)
    flat = [b for p in places for b in p]
    ins = [(p, WHOLE) for p in pieces]
    if before is not None:
        ins.append((before, WHOLE))
    nacc = len(ins)
    if finish is not None:
        level, y, inv, inv_other = finish
        ins += [(y, WHOLE), (inv, HBM), (inv_other, HBM)]
        outs = [PAIR, TILE, TILE]
    else:
        outs = [(nsrc * BLK, HALF)]
    nf = len(ins)
    ins += [(a, WHOLE) for a in sources]
    nin = len(ins)

    def body(tab, *refs):
        in_refs, out_refs = refs[:nin], refs[nin : nin + len(outs)]
        c = tab[CORE]
        if finish is not None:
            small = refs[nin + len(outs) :]
            smalls = small_start(level, c, (), in_refs[nacc + 1 : nf], small)
        rows = [p[...].reshape(-1, HALF) for p in in_refs[:npiece]]
        pair = paired(jnp.concatenate(rows, axis=0))
        wide = [
            jnp.concatenate([u[:, window_of(tab, b)] for u in in_refs[nf:]], axis=0)
            for b in flat
        ]
        high, low = split(jnp.concatenate(wide, axis=1))
        total = jnp.dot(high, pair, preferred_element_type=F32)
        total = total + jnp.dot(low, pair, preferred_element_type=F32)
        total = total[:, :HALF] + total[:, HALF:]
        if before is not None:
            total = total + in_refs[npiece][...]
        if finish is None:
            out_refs[0][...] = total
            return
        x_ref, mine_ref, send_ref = out_refs
        y_ref = in_refs[nacc]
        wait_all(smalls)
        for n, (idx, part) in enumerate(((c, mine_ref), (1 - c, send_ref))):
            x = exact(small[1][n], y_ref[idx] - total[n * BLK : (n + 1) * BLK])
            x_ref[idx] = x
            part[...] = x

    return run(body, table, ins, outs, SMALL_SCRATCH if finish is not None else [])


def assemble(table, mine, received):
    def body(tab, *refs):
        out = refs[8]
        for k in range(4):
            a, b = refs[k][...], refs[4 + k][...]
            first = tab[CORE] == 0
            out[k, :, :HALF] = jnp.where(first, a, b)
            out[k, :, HALF:] = jnp.where(first, b, a)

    ins = [(a, WHOLE) for a in mine + received]
    return run(body, table, ins, [(4, BLK, 2 * HALF)])[0]


def make_table(leaf, panel):
    z, y = leaf // NY, leaf % NY
    x, c = panel // 2, panel % 2
    u = jnp.where(c == 0, x, y)
    v = jnp.where(c == 0, y, x)
    four = jnp.arange(4, dtype=jnp.int32)
    ur, vr = jnp.repeat(four, 4), jnp.tile(four, 4)

    def offset(orders, k):
        a = jnp.array([o[k] for o in orders[0]] + [0], jnp.int32)
        b = jnp.array([o[k] for o in orders[1]] + [0], jnp.int32)
        return jnp.where(c == 0, a, b)

    dy, dx = [offset((OUTWARD, OUTWARD_1), k) for k in (0, 1)]
    ey, ex = [offset((OFFSETS, OFFSETS_1), k) for k in (0, 1)]

    def plane(up, vp):
        return jnp.where(c == 0, vp * NX + up, up * NX + vp)

    parts = [
        jnp.stack([c, z % 2]),
        (v + four) % 4,
        ((y ^ dy) & 1) * NX + (x + dx) % NX,
        ((y ^ ey) & 1) * NX + (x - ex + NX) % NX,
        plane((u + ur) % 4, vr),
        plane((u - ur + 4) % 4, (v - vr + 4) % 4),
    ]
    return jnp.concatenate([p.astype(jnp.int32) for p in parts])


def after(value, other):
    return lax.optimization_barrier((value, other))[0]


def local(
    rhs,
    lower_inv,
    upper_inv,
    lower_coupling_1,
    lower_coupling_2,
    lower_coupling_3,
    upper_coupling_1,
    upper_coupling_2,
    upper_coupling_3,
):
    leaf, panel = lax.axis_index("leaf"), lax.axis_index("panel")
    table = make_table(leaf, panel)

    def held(a):
        return jnp.where(panel >= 0, a, 0.0)

    rhs_o = to_core(rhs)
    low_o = to_core(lower_inv)
    l1_o = to_core(lower_coupling_1)
    lows = (held(rhs), rhs_o, held(lower_inv), low_o)
    y0, *parts = forward_step(
        table,
        (0, []) + lows,
        [],
        [lower_coupling_1, l1_o],
        [[(BLK1 + j, 0)] for j in range(8)],
    )
    l2_o = to_core(after(lower_coupling_2, y0))
    pieces = [parts[7]] + [near(parts[j], (OUTWARD, OUTWARD_1), j) for j in range(7)]

    def along_v(pieces):
        got = {r: shift_v(pieces[r], r) for r in (2, 3, 1)}
        return [pieces[0], got[1], got[2], got[3]]

    def across(halves):
        return along_v(sum_step(table, halves))

    def across_z(halves):
        pieces = along_v(pair_step(table, halves))
        return [to_z(cross_step(table, pieces))] + pieces

    def spread(finish, ys, sources, first, second):
        out = forward_step(table, finish, ys, sources, [first[2], second[2]])
        a2, b2 = shift_u(out[-2], 1), shift_u(out[-1], -1)
        if finish is not None:
            ys = [out[0]]
        d1, d3 = forward_step(table, None, ys, sources, [second[1], first[3]])
        d1, d3 = shift_u(d1, 1), shift_u(d3, -1)
        s1, s3 = forward_step(table, None, ys, sources, [first[1], second[3]])
        s1, s3 = add_step(table, [(s1, a2), (s3, b2)])
        s1, s3 = shift_u(s1, 1), shift_u(s3, -1)
        a0, b0 = forward_step(table, None, ys, sources, [first[0], second[0]])
        halves = [[a0, d3, s1], [b0, d1, s3]]
        return ys[0], across(halves) if a0.shape[0] == 2 else across_z(halves)

    def half_plane(base, columns, z):
        return [[(base + ur * 4 + v, z) for v in columns] for ur in range(4)]

    y1, pieces = spread(
        (1, pieces) + lows,
        [],
        [lower_coupling_2, l2_o],
        half_plane(BLK2, (0, 1), 0),
        half_plane(BLK2, (2, 3), 0),
    )
    l3_o = to_core(after(lower_coupling_3, y1))
    up_o = to_core(after(upper_inv, y1))
    y2, pieces = spread(
        (2, pieces) + lows,
        [],
        [lower_coupling_3, l3_o],
        half_plane(BLK2, range(4), 1),
        half_plane(BLK2, range(4), 2),
    )
    u3_o = to_core(after(upper_coupling_3, y2))
    x3, mine3, send3 = top_step(table, pieces, *lows, upper_inv, up_o)
    got3 = to_core(send3)
    u2_o = to_core(after(upper_coupling_2, x3))

    def around_halves(a, b):
        a1, a3 = shift_u(a, 1), shift_u(a, -1)
        b1, b3 = shift_u(b, 1), shift_u(b, -1)
        return [a, a1, shift_u(a1, 1), a3], [b, b1, shift_u(b3, -1), b3]

    def gathered(groups, sources, finish):
        acc = None
        for i, group in enumerate(groups):
            last = finish if i == len(groups) - 1 else None
            arrays, places = zip(*group)
            out = backward_step(table, acc, arrays, places, sources, last)
            acc = out[0]
        return out

    line = jnp.stack(along_v([x3] * 4))
    own, other = around_halves(line, to_z(line))
    own = list(zip(own, half_plane(KBLK2, range(4), 1)))
    other = list(zip(other, half_plane(KBLK2, range(4), 2)))
    x2, mine2, send2 = gathered(
        [[g[0] for g in (own, other)], own[1::2] + other[1::2], own[2:3] + other[2:3]],
        [upper_coupling_3, u3_o],
        (2, y2, upper_inv, up_o),
    )
    got2 = to_core(send2)
    u1_o = to_core(after(upper_coupling_1, x2))
    line = along_v([x2] * 4)
    near_v, far_v = around_halves(jnp.stack(line[:2]), jnp.stack(line[2:]))
    near_v = list(zip(near_v, half_plane(KBLK2, (0, 1), 0)))
    far_v = list(zip(far_v, half_plane(KBLK2, (2, 3), 0)))
    x1, mine1, send1 = gathered(
        [near_v[:1] + far_v[:1], near_v[1::2] + far_v[1::2], near_v[2:3] + far_v[2:3]],
        [upper_coupling_2, u2_o],
        (1, y1, upper_inv, up_o),
    )
    got1 = to_core(send1)

    sources = [upper_coupling_1, u1_o]
    arrivals = [near(x1, (OFFSETS, OFFSETS_1), j) for j in range(7)]
    places = [[(KBLK1 + j, 0)] for j in range(8)]
    (acc,) = backward_step(table, None, [x1], places[7:], sources, None)
    (acc,) = backward_step(table, acc, arrivals[:4], places[:4], sources, None)
    _, mine0, send0 = backward_step(
        table, acc, arrivals[4:], places[4:7], sources, (0, y0, upper_inv, up_o)
    )
    got0 = to_core(send0)
    return assemble(table, [mine0, mine1, mine2, mine3], [got0, got1, got2, got3])


def solution(mesh):
    return jax.shard_map(
        local,
        mesh=mesh,
        in_specs=(
            P(None, ("leaf", "panel"), None),
            P(None, ("leaf", "panel"), None),
            P(None, ("leaf", "panel"), None),
            P(None, ("leaf", "panel")),
            P(None, ("leaf", "panel")),
            P(None, ("leaf", "panel")),
            P(("leaf", "panel"), None),
            P(("leaf", "panel"), None),
            P(("leaf", "panel"), None),
        ),
        out_specs=P(None, ("leaf", "panel"), None),
        check_vma=False,
    )
```
